256 devices in a mesh: ctx: 64 (over x, z, core), head: 4 (over y).
Axes of the slice: x: 4, y: 4, z: 8, core: 2. Of those that a mesh axis runs over, the one named last changes fastest.
Arguments:
- queries: bfloat16 [16384, 4096], P('ctx', 'head'), may hold values from -5 to 5
- keys: bfloat16 [16384, 4096], P('ctx', 'head'), may hold values from -5 to 5
- values: bfloat16 [16384, 4096], P('ctx', 'head'), may hold values from -6 to 6
- grad_out: bfloat16 [16384, 4096], P('ctx', 'head'), may hold values from -6 to 6
- cluster_ids: int32 [32, 16384, 1], P(None, ('ctx', 'head')), may hold values from 0 to 255; in each aligned block of 256 rows (0 to 255, 256 to 511, ..., all dimensions but the last counted through in order) at most 2 rows name the same one
Outputs:
- attended: bfloat16 [16384, 4096], P('ctx', 'head')
- grad_queries: bfloat16 [16384, 4096], P('ctx', 'head')
- grad_keys: bfloat16 [16384, 4096], P('ctx', 'head')
- grad_values: bfloat16 [16384, 4096], P('ctx', 'head')
The draws below stay inside these ranges and needn't reach their ends.
Inputs may be any that keep to these rules, and one draw needn't show every extreme that they name: `cluster_ids`: for every head, among the 256 tokens of any aligned block (tokens k * 256 to (k + 1) * 256 - 1) no cluster is named more than 2 times, and in every draw some cluster of some block is named exactly 2 times.
All inputs are finite; a program needn't handle non-finite values.
Results may differ from the reference program's by a relative error of at most 0.012.
Values may be sent and summed in bfloat16 or wider, within the bound.
A program may use at most 64 MiB of HBM per device.

```python
import math
import jax
import jax.numpy as jnp
import numpy as np
from jax import lax

HEADS = 32
HEAD_DIM = 128
CLUSTERS = 256
WINDOW = 256
TOK_DEV = 256
SLOTS = 2
TOKENS = 16384
N_CTX = 64


def paired_rows(key):
    base = jax.random.fold_in(key, 7)
    streams = jax.random.split(base, 3)
    shape = (TOKENS, HEADS * HEAD_DIM)
    first = jnp.clip(jax.random.normal(streams[1], shape), -4.5, 4.5)
    second = jnp.clip(jax.random.normal(streams[2], shape), -4.5, 4.5)
    return (first, second)


def draw_queries(key, part):
    return paired_rows(key)[0].astype(jnp.bfloat16)


def draw_keys(key, part):
    return paired_rows(key)[1].astype(jnp.bfloat16)


def level_of(own_key, shape, cuts, smallest, high):
    def one(axis_at, blocks):
        draws = jax.random.uniform(jax.random.fold_in(jax.random.fold_in(own_key, 6), axis_at), (blocks,), jnp.float32, smallest / len(cuts), high / len(cuts))
        return jnp.repeat(jnp.exp(draws), shape[axis_at] // blocks).reshape((-1,) + (1,) * (len(shape) - axis_at - 1))

    factor_of = one(*cuts[0])
    for cut in cuts[1:]:
        factor_of = factor_of * one(*cut)
    return factor_of


def routed_block(stream_key, own, number, rows, amount, top, limit, slope):
    order = jax.random.permutation(stream_key, amount)
    heavy_load, ordinary = load_shares(amount, rows * top, limit, slope, True), load_shares(amount, rows * top, limit, slope, False)
    places = jnp.arange(amount)

    def named(tallies, turn):
        used = int((tallies > 0).sum())
        fixed = max(1, used // 4)
        shifted = fixed + (places - fixed + turn * (used - fixed)) % max(1, amount - fixed)
        return jnp.zeros((amount,), jnp.int32).at[order[jnp.where(places < fixed, places, shifted)]].set(jnp.asarray(tallies, jnp.int32))

    tallies = jnp.where(number % 4 == 0, named(heavy_load, number // 4), named(ordinary, number - number // 4 - 1))
    mixed = jax.random.permutation(jax.random.fold_in(own, 3), amount)
    donor, sink = mixed[0:amount // 2 * 2:2], mixed[1:amount // 2 * 2:2]
    room = jnp.minimum(tallies[donor] - 1, limit - tallies[sink]) // 2
    room = jnp.where((donor == order[0]) | (sink == order[0]) | (tallies[sink] == 0), 0, jnp.maximum(room, 0))
    shifted = jax.random.randint(jax.random.fold_in(own, 4), (amount // 2,), 0, 1 << 20) % (room + 1)
    tallies = tallies.at[donor].add(-shifted).at[sink].add(shifted)
    items = jnp.searchsorted(jnp.cumsum(tallies), jnp.arange(rows * top), side="right").astype(jnp.int32)
    grid = items.reshape(top, rows).T
    grid = grid[jax.random.permutation(jax.random.fold_in(own, 1), rows)]
    turn = jax.random.randint(jax.random.fold_in(own, 2), (rows, 1), 0, top)
    return jnp.take_along_axis(grid, (jnp.arange(top)[None, :] + turn) % top, axis=1)


def load_shares(amount, total, limit, slope, full):
    portions = [(1 << 20) // math.isqrt(standing ** slope) + 1 for standing in range(1, amount + 1)]
    largest = limit if full else min(limit, max(-(-total // amount), total * portions[0] // sum(portions)))
    least = 1 if total - largest >= amount - 1 else 0
    given, spare = [largest] + [least] * (amount - 1), total - largest - least * (amount - 1)
    while spare > 0:
        movable = [i for i in range(1, amount) if given[i] < largest] or [i for i in range(1, amount) if given[i] < limit]
        mass, remaining = sum([portions[i] for i in movable]), spare
        for i in movable:
            more = min(limit - given[i], max(1, remaining * portions[i] // mass), spare)
            given[i] = given[i] + more
            spare = spare - more
    return np.array(given)


def gaussian(rng, extent, width, limit, shards=(), kind=jnp.bfloat16):
    entries = jax.random.normal(rng, extent, jnp.float32) * width
    if len(shards) > 0:
        entries = level_of(rng, extent, shards, -0.22, 0.18) * entries
    return jnp.clip(entries, min=-limit, max=limit).astype(kind)


def setup_inputs(seed: int = 0) -> dict:
    key_list = jax.random.split(jax.random.key(seed), 6)
    queries = draw_queries(jax.random.fold_in(key_list[5], 71), 0)
    keys = draw_keys(jax.random.fold_in(key_list[5], 71), 0)
    values = gaussian(key_list[2], (TOKENS, HEADS * HEAD_DIM), 1.0, 6.0, ((0, 64), (1, 4)))
    grad_out = gaussian(key_list[3], (TOKENS, HEADS * HEAD_DIM), 1.0, 6.0, ((0, 64), (1, 4)))
    cluster_ids_keys = jax.random.split(jax.random.fold_in(key_list[4], 1), HEADS * TOKENS // TOK_DEV)
    cluster_ids_turns = jax.random.permutation(jax.random.fold_in(key_list[4], 3), HEADS * TOKENS // TOK_DEV)
    cluster_ids = jax.vmap(lambda own, number: routed_block(jax.random.fold_in(key_list[4], 2), own, number, TOK_DEV, CLUSTERS, 1, SLOTS, 2))(cluster_ids_keys, cluster_ids_turns).reshape((HEADS, TOKENS, 1))
    return dict(queries=queries, keys=keys, values=values, grad_out=grad_out, cluster_ids=cluster_ids)


NEG_LARGE = -1.0e30


def soft_weights(scores, allowed, floored):
    masked = jnp.where(allowed, scores, NEG_LARGE)
    top = jnp.max(masked, axis=-1, keepdims=True)
    total = jnp.sum(jnp.where(allowed, jnp.exp(masked - top), 0.0), axis=-1, keepdims=True)
    if floored:
        total = jnp.maximum(total, 1.0)
    log_total = top + jnp.log(total)
    weights = jnp.where(allowed, jnp.exp(masked - log_total), 0.0).astype(jnp.bfloat16)
    return weights


def window_head(query, key_rows, value_rows, grad_rows):
    score_scale = HEAD_DIM ** -0.5
    count_blocks = TOKENS // WINDOW
    zero_rows = jnp.zeros((WINDOW, HEAD_DIM), key_rows.dtype)
    key_pad = jnp.concatenate([zero_rows, key_rows], axis=0)
    value_pad = jnp.concatenate([zero_rows, value_rows], axis=0)
    query_index = jnp.arange(WINDOW, dtype=jnp.int32)[:, None]
    key_index = jnp.arange(2 * WINDOW, dtype=jnp.int32)[None, :]

    def step(carry, block):
        grad_key_pad, grad_value_pad = carry
        offset = (block * WINDOW).astype(jnp.int32)
        query_block = lax.dynamic_slice_in_dim(query, offset, WINDOW, 0)
        grad_block = lax.dynamic_slice_in_dim(grad_rows, offset, WINDOW, 0)
        key_block = lax.dynamic_slice_in_dim(key_pad, offset, 2 * WINDOW, 0)
        value_block = lax.dynamic_slice_in_dim(value_pad, offset, 2 * WINDOW, 0)
        allowed = (key_index <= query_index + WINDOW) & (key_index > query_index) & (offset - WINDOW + key_index >= 0)
        scores = jnp.dot(query_block, key_block.T, preferred_element_type=jnp.float32) * score_scale
        weights = soft_weights(scores, allowed, False)
        attended = jnp.dot(weights, value_block, preferred_element_type=jnp.float32)
        grad_weights = jnp.dot(grad_block, value_block.T, preferred_element_type=jnp.float32)
        row_dot = jnp.sum(grad_block.astype(jnp.float32) * attended, axis=1, keepdims=True)
        grad_scores = (weights.astype(jnp.float32) * (grad_weights - row_dot)).astype(jnp.bfloat16)
        grad_query = jnp.dot(grad_scores, key_block, preferred_element_type=jnp.float32) * score_scale
        grad_key = jnp.dot(grad_scores.T, query_block, preferred_element_type=jnp.float32) * score_scale
        grad_value = jnp.dot(weights.T, grad_block, preferred_element_type=jnp.float32)
        old_key = lax.dynamic_slice_in_dim(grad_key_pad, offset, 2 * WINDOW, 0)
        old_value = lax.dynamic_slice_in_dim(grad_value_pad, offset, 2 * WINDOW, 0)
        grad_key_pad = lax.dynamic_update_slice_in_dim(grad_key_pad, old_key + grad_key, offset, 0)
        grad_value_pad = lax.dynamic_update_slice_in_dim(grad_value_pad, old_value + grad_value, offset, 0)
        return (grad_key_pad, grad_value_pad), (attended, grad_query)

    start = (jnp.zeros((TOKENS + WINDOW, HEAD_DIM), jnp.float32), jnp.zeros((TOKENS + WINDOW, HEAD_DIM), jnp.float32))
    (grad_key_pad, grad_value_pad), (attended, grad_query) = lax.scan(step, start, jnp.arange(count_blocks, dtype=jnp.int32))
    return (attended.reshape(TOKENS, HEAD_DIM), grad_query.reshape(TOKENS, HEAD_DIM),
            grad_key_pad[WINDOW:], grad_value_pad[WINDOW:])


def cluster_head(query, key_rows, value_rows, grad_rows, cluster_row):
    score_scale = HEAD_DIM ** -0.5
    capacity = SLOTS * N_CTX
    count_blocks = TOKENS // TOK_DEV
    grouped = cluster_row.reshape(count_blocks, TOK_DEV)
    position = jnp.arange(TOK_DEV, dtype=jnp.int32)
    earlier = (grouped[:, :, None] == grouped[:, None, :]) & (position[None, None, :] < position[None, :, None])
    rank = jnp.sum(earlier.astype(jnp.int32), axis=2)
    source = jnp.arange(count_blocks, dtype=jnp.int32)[:, None]
    target = (grouped * capacity + source * SLOTS + rank).reshape(TOKENS).astype(jnp.int32)

    def place(rows):
        empty = jnp.zeros((CLUSTERS * capacity, HEAD_DIM), rows.dtype)
        return empty.at[target].set(rows).reshape(CLUSTERS, capacity, HEAD_DIM).astype(jnp.float32)

    filled = jnp.zeros((CLUSTERS * capacity,), jnp.int32).at[target].set(1).reshape(CLUSTERS, capacity) > 0
    slot_order = jnp.arange(capacity, dtype=jnp.int32)
    allowed = filled[:, None, :] & (slot_order[None, :] <= slot_order[:, None])[None, :, :]
    query_slots = place(query)
    key_slots = place(key_rows)
    value_slots = place(value_rows)
    grad_slots = place(grad_rows)
    scores = jnp.einsum("cad,cbd->cab", query_slots, key_slots) * score_scale
    weights = soft_weights(scores, allowed, True).astype(jnp.float32)
    attended = jnp.einsum("cab,cbd->cad", weights, value_slots)
    grad_weights = jnp.einsum("cad,cbd->cab", grad_slots, value_slots)
    row_dot = jnp.sum(grad_slots * attended, axis=2, keepdims=True)
    grad_scores = (weights * (grad_weights - row_dot)).astype(jnp.bfloat16).astype(jnp.float32)
    grad_query = jnp.einsum("cab,cbd->cad", grad_scores, key_slots) * score_scale
    grad_key = jnp.einsum("cab,cad->cbd", grad_scores, query_slots) * score_scale
    grad_value = jnp.einsum("cab,cad->cbd", weights, grad_slots)

    def pick(tensor):
        return tensor.reshape(CLUSTERS * capacity, HEAD_DIM)[target].astype(jnp.bfloat16)

    return pick(attended), pick(grad_query), pick(grad_key), pick(grad_value)


def reference(queries, keys, values, grad_out, cluster_ids):
    def per_head(matrix):
        return matrix.reshape(TOKENS, HEADS, HEAD_DIM).transpose(1, 0, 2)

    def one_head(inputs):
        query, key_rows, value_rows, grad_rows, cluster_row = inputs
        local_parts = window_head(query, key_rows, value_rows, grad_rows)
        cluster_parts = cluster_head(query, key_rows, value_rows, grad_rows, cluster_row)
        return tuple((local_parts[index] + cluster_parts[index].astype(jnp.float32)).astype(jnp.bfloat16) for index in range(4))

    results = lax.map(one_head, (per_head(queries), per_head(keys), per_head(values), per_head(grad_out), cluster_ids[:, :, 0]))

    def join(tensor):
        return tensor.transpose(1, 0, 2).reshape(TOKENS, HEADS * HEAD_DIM)

    return (join(results[0]), join(results[1]), join(results[2]), join(results[3]))
```

```python
import functools

import jax
import jax.numpy as jnp
from jax import lax
from jax.experimental import pallas as pl
from jax.experimental.pallas import tpu as pltpu
from jax.sharding import PartitionSpec as P

HEAD_DIM = 128
CLUSTERS = 256
WINDOW = 256
SLOTS = 2
NEG_LARGE = -1e30
EMPTY_KEY = 64.0
MESH = pl.DeviceIdType.MESH
SCALE = HEAD_DIM**-0.5
F32 = jnp.float32
BF16 = jnp.bfloat16


def nt(a, b):
    return lax.dot_general(a, b, (((1,), (1,)), ((), ())), preferred_element_type=F32)


def tn(a, b):
    return lax.dot_general(a, b, (((0,), (0,)), ((), ())), preferred_element_type=F32)


def nn(a, b):
    return jnp.dot(a, b, preferred_element_type=F32)


def attend(query, key, value, grad, allowed):
    scores = jnp.where(allowed, nt(query, key) * SCALE, NEG_LARGE)
    top = jnp.max(scores, axis=-1, keepdims=True)
    exps = jnp.where(allowed, jnp.exp(scores - top), 0.0)
    total = jnp.maximum(jnp.sum(exps, axis=-1, keepdims=True), 1.0)
    weights = exps * (1.0 / total)
    weights16 = weights.astype(BF16)
    attended = nn(weights16, value)
    row_dot = jnp.sum(grad.astype(F32) * attended, axis=-1, keepdims=True)
    grad_scores = (weights16.astype(F32) * (nt(grad, value) - row_dot)).astype(BF16)
    grad_query = nn(grad_scores, key) * SCALE
    grad_key = tn(grad_scores, query) * SCALE
    grad_value = tn(weights16, grad)
    return attended, grad_query, grad_key, grad_value


def kernel(
    owners, peers, heads, rows,
    q_ref, k_ref, v_ref, g_ref, ids_ref,
    out_o, out_q, out_k, out_v,
    sbuf, rbuf, bsend, brecv, halo, hsend, hrecv, win, idr, crow, ccol, tcol,
    id_sem, halo_sem, hback_sem, send_sem, recv_sem, bsend_sem, brecv_sem,
):
    me = lax.axis_index("ctx")
    my_head = lax.axis_index("head")
    nxt = lax.rem(me + 1, owners)
    prv = lax.rem(me + owners - 1, owners)
    pairs = heads // 2
    each = CLUSTERS // owners
    slot_rows = owners * SLOTS * 2 * each
    pair_rows = 2 * rows

    barrier = pltpu.get_barrier_semaphore()

    def greet(i, c):
        pl.semaphore_signal(barrier, inc=1, device_id={"ctx": lax.rem(me + i, owners)}, device_id_type=MESH)
        return c

    lax.fori_loop(1, owners, greet, 0)
    for i in range(1, peers):
        pl.semaphore_signal(barrier, inc=1, device_id={"head": lax.rem(my_head + i, peers)}, device_id_type=MESH)
    pl.semaphore_wait(barrier, owners - 1 + peers - 1)

    id_copies = []
    for i in range(1, peers):
        peer = lax.rem(my_head + i, peers)
        copy = pltpu.make_async_remote_copy(
            src_ref=ids_ref.at[peer], dst_ref=idr.at[i - 1],
            send_sem=id_sem.at[0, i - 1], recv_sem=id_sem.at[1, i - 1],
            device_id={"head": peer}, device_id_type=MESH,
        )
        copy.start()
        id_copies.append(copy)
    halo_copies = []
    for i, ref in enumerate((k_ref, v_ref)):
        copy = pltpu.make_async_remote_copy(
            src_ref=ref, dst_ref=halo.at[i], send_sem=halo_sem.at[0, i], recv_sem=halo_sem.at[1, i],
            device_id={"ctx": nxt}, device_id_type=MESH,
        )
        copy.start()
        halo_copies.append(copy)
    for copy in id_copies:
        copy.wait()
    ids = ids_ref[my_head]
    for i in range(1, peers):
        ids = ids + idr[i - 1]
    head_row = lax.broadcasted_iota(jnp.int32, (heads, rows), 0)
    spot = (ids * (1 + 36 * head_row)) & (CLUSTERS - 1)
    eye = (
        lax.broadcasted_iota(jnp.int32, (rows, rows), 0) == lax.broadcasted_iota(jnp.int32, (rows, rows), 1)
    ).astype(BF16)
    spot_t = nt(eye, spot.astype(F32).astype(BF16)).astype(jnp.int32)
    for h in range(heads):
        crow[h] = spot[h : h + 1, :]
        ccol[h] = spot_t[:, h : h + 1]

    sub_tok = lax.broadcasted_iota(jnp.int32, (rows, rows), 0)
    lane_tok = lax.broadcasted_iota(jnp.int32, (rows, rows), 1)

    def place(spots, rank, hh):
        return (spots // each) * (SLOTS * 2 * each) + rank * (2 * each) + hh * each + spots % each

    def columns(h):
        return pl.ds(pl.multiple_of(h * HEAD_DIM, HEAD_DIM), HEAD_DIM)

    def build(p, c):
        lanes, tokens = [], []
        for hh in range(2):
            h = 2 * p + hh
            row, col = crow[h], ccol[h]
            same = col == row
            rank_row = jnp.sum(jnp.where(same & (sub_tok < lane_tok), 1.0, 0.0), axis=0, keepdims=True)
            rank_col = jnp.sum(jnp.where(same & (lane_tok < sub_tok), 1.0, 0.0), axis=1, keepdims=True)
            lanes.append(place(row, rank_row.astype(jnp.int32), hh))
            tcol[h] = place(col, rank_col.astype(jnp.int32), hh)
            tokens.append(jnp.concatenate([r[:, columns(h)] for r in (q_ref, k_ref, v_ref, g_ref)], axis=1))
        lane = jnp.concatenate(lanes, axis=1)
        token = jnp.concatenate(tokens, axis=0)
        hit = lax.broadcasted_iota(jnp.int32, (slot_rows, pair_rows), 0) == lane
        one_hot = jnp.where(hit, 1.0, 0.0)
        empty = jnp.where(jnp.sum(one_hot, axis=1, keepdims=True) > 0.5, 0.0, EMPTY_KEY)
        filled = nn(one_hot.astype(BF16), token)
        key_lane = lax.broadcasted_iota(jnp.int32, (1, 4 * HEAD_DIM), 1)
        mark = jnp.where((key_lane >= HEAD_DIM) & (key_lane < 2 * HEAD_DIM), 1.0, 0.0)
        filled = filled + empty * mark
        sbuf[p] = filled.astype(BF16).reshape(owners, SLOTS, 2 * each, 4 * HEAD_DIM)

        def send(i, c):
            dst = lax.rem(me + i, owners)
            pltpu.make_async_remote_copy(
                src_ref=sbuf.at[p, dst], dst_ref=rbuf.at[p, me], send_sem=send_sem.at[p], recv_sem=recv_sem.at[p],
                device_id={"ctx": dst}, device_id_type=MESH,
            ).start()
            return c

        lax.fori_loop(1, owners, send, 0)
        pltpu.make_async_copy(sbuf.at[p, me], rbuf.at[p, me], recv_sem.at[p]).start()
        return c

    lax.fori_loop(0, pairs, build, 0)

    for copy in halo_copies:
        copy.wait()
    q_pos = lax.broadcasted_iota(jnp.int32, (rows, WINDOW + rows), 0)
    k_pos = lax.broadcasted_iota(jnp.int32, (rows, WINDOW + rows), 1) - WINDOW
    in_window = (k_pos <= q_pos) & (k_pos > q_pos - WINDOW) & (k_pos + me * rows >= 0)

    def window(h, c):
        cols = columns(h)
        key_all = jnp.concatenate([halo[0, :, cols], k_ref[:, cols]], axis=0)
        value_all = jnp.concatenate([halo[1, :, cols], v_ref[:, cols]], axis=0)
        att, gq, gk, gv = attend(q_ref[:, cols], key_all, value_all, g_ref[:, cols], in_window)
        win[0, :, cols] = att
        win[1, :, cols] = gq
        win[2, :, cols] = gk[WINDOW:]
        win[3, :, cols] = gv[WINDOW:]
        hsend[0, :, cols] = gk[:WINDOW].astype(BF16)
        hsend[1, :, cols] = gv[:WINDOW].astype(BF16)
        return c

    lax.fori_loop(0, heads, window, 0)
    back_copies = []
    for i in range(2):
        copy = pltpu.make_async_remote_copy(
            src_ref=hsend.at[i], dst_ref=hrecv.at[i], send_sem=hback_sem.at[0, i], recv_sem=hback_sem.at[1, i],
            device_id={"ctx": prv}, device_id_type=MESH,
        )
        copy.start()
        back_copies.append(copy)

    groups = 2 * each
    part = owners * groups
    p_row = lax.broadcasted_iota(jnp.int32, (part, part), 0)
    p_col = lax.broadcasted_iota(jnp.int32, (part, part), 1)
    to_group = jnp.where(p_col == (p_row % owners) * groups + p_row // owners, 1.0, 0.0).astype(BF16)
    from_group = jnp.where(p_col == (p_row % groups) * owners + p_row // groups, 1.0, 0.0).astype(BF16)
    capacity = owners * SLOTS
    a_pos = lax.broadcasted_iota(jnp.int32, (capacity, capacity), 0)
    b_pos = lax.broadcasted_iota(jnp.int32, (capacity, capacity), 1)
    causal = (b_pos % owners) * SLOTS + b_pos // owners <= (a_pos % owners) * SLOTS + a_pos // owners
    first = jnp.where(lax.broadcasted_iota(jnp.int32, (8, HEAD_DIM), 1) == 0, 1.0, 0.0).astype(BF16)

    def cluster(p, c):
        pltpu.make_async_copy(rbuf.at[p], rbuf.at[p], recv_sem.at[p]).wait()
        slots = [
            nn(to_group, rbuf[p, :, r].reshape(part, 4 * HEAD_DIM)).astype(BF16) for r in range(SLOTS)
        ]
        results = [[], []]
        for g in range(groups):
            packed = jnp.concatenate([s[g * owners : (g + 1) * owners] for s in slots], axis=0)
            query, key, value, grad = (packed[:, i * HEAD_DIM : (i + 1) * HEAD_DIM] for i in range(4))
            valid = nt(first, key)[0:1, :] < EMPTY_KEY / 2
            done = attend(query, key, value, grad, causal & valid)
            done = jnp.concatenate([d.astype(BF16) for d in done], axis=1)
            for r in range(SLOTS):
                results[r].append(done[r * owners : (r + 1) * owners])
        for r in range(SLOTS):
            back = nn(from_group, jnp.concatenate(results[r], axis=0)).astype(BF16)
            bsend[p, :, r] = back.reshape(owners, groups, 4 * HEAD_DIM)

        def send(i, c):
            dst = lax.rem(me + i, owners)
            pltpu.make_async_remote_copy(
                src_ref=bsend.at[p, dst], dst_ref=brecv.at[p, me], send_sem=bsend_sem.at[p],
                recv_sem=brecv_sem.at[p], device_id={"ctx": dst}, device_id_type=MESH,
            ).start()
            return c

        lax.fori_loop(1, owners, send, 0)
        pltpu.make_async_copy(bsend.at[p, me], brecv.at[p, me], brecv_sem.at[p]).start()
        return c

    lax.fori_loop(0, pairs, cluster, 0)

    for copy in back_copies:
        copy.wait()

    def finish(p, c):
        pltpu.make_async_copy(brecv.at[p], brecv.at[p], brecv_sem.at[p]).wait()
        target = jnp.concatenate([tcol[2 * p], tcol[2 * p + 1]], axis=0)
        hit = lax.broadcasted_iota(jnp.int32, (pair_rows, slot_rows), 1) == target
        mine = nn(jnp.where(hit, 1.0, 0.0).astype(BF16), brecv[p].reshape(slot_rows, 4 * HEAD_DIM))
        for hh in range(2):
            cols = columns(2 * p + hh)
            part_of = [mine[hh * rows : (hh + 1) * rows, i * HEAD_DIM : (i + 1) * HEAD_DIM] for i in range(4)]
            out_o[:, cols] = (win[0, :, cols] + part_of[0]).astype(BF16)
            out_q[:, cols] = (win[1, :, cols] + part_of[1]).astype(BF16)
            out_k[:, cols] = (win[2, :, cols] + hrecv[0, :, cols].astype(F32) + part_of[2]).astype(BF16)
            out_v[:, cols] = (win[3, :, cols] + hrecv[1, :, cols].astype(F32) + part_of[3]).astype(BF16)
        return c

    lax.fori_loop(0, pairs, finish, 0)

    def drain(p, c):
        pltpu.make_async_copy(sbuf.at[p, pl.ds(0, owners - 1)], sbuf.at[p, pl.ds(0, owners - 1)], send_sem.at[p]).wait()
        pltpu.make_async_copy(bsend.at[p, pl.ds(0, owners - 1)], bsend.at[p, pl.ds(0, owners - 1)], bsend_sem.at[p]).wait()
        return c

    lax.fori_loop(0, pairs, drain, 0)


def on_device(queries, keys, values, grad_out, cluster_ids):
    rows, width = queries.shape
    heads = width // HEAD_DIM
    owners = lax.axis_size("ctx")
    peers = lax.axis_size("head")
    each = CLUSTERS // owners
    share = rows // peers
    ids = cluster_ids[:, :, 0].reshape(peers, heads, share)
    spread = jnp.zeros((peers, heads, rows), jnp.int32)
    spread = lax.dynamic_update_slice_in_dim(spread, ids, lax.axis_index("head") * share, axis=2)
    pairs = heads // 2
    buffer = pltpu.VMEM((pairs, owners, SLOTS, 2 * each, 4 * HEAD_DIM), BF16)
    vmem = pl.BlockSpec(memory_space=pltpu.VMEM)
    dma = pltpu.SemaphoreType.DMA
    return pl.pallas_call(
        functools.partial(kernel, owners, peers, heads, rows),
        out_shape=[jax.ShapeDtypeStruct((rows, width), BF16)] * 4,
        in_specs=[vmem] * 5,
        out_specs=[vmem] * 4,
        scratch_shapes=[
            buffer, buffer, buffer, buffer,
            pltpu.VMEM((2, WINDOW, width), BF16),
            pltpu.VMEM((2, WINDOW, width), BF16),
            pltpu.VMEM((2, WINDOW, width), BF16),
            pltpu.VMEM((4, rows, width), F32),
            pltpu.VMEM((peers - 1, heads, rows), jnp.int32),
            pltpu.VMEM((heads, 1, rows), jnp.int32),
            pltpu.VMEM((heads, rows, 1), jnp.int32),
            pltpu.VMEM((heads, rows, 1), jnp.int32),
            dma((2, peers - 1)), dma((2, 2)), dma((2, 2)),
            dma((pairs,)), dma((pairs,)), dma((pairs,)), dma((pairs,)),
        ],
        compiler_params=pltpu.CompilerParams(
            collective_id=0, has_side_effects=True, vmem_limit_bytes=60 * 1024 * 1024
        ),
    )(queries, keys, values, grad_out, spread)


def solution(mesh):
    return jax.shard_map(
        on_device,
        mesh=mesh,
        in_specs=(
            P("ctx", "head"), P("ctx", "head"), P("ctx", "head"), P("ctx", "head"),
            P(None, ("ctx", "head"), None),
        ),
        out_specs=(P("ctx", "head"),) * 4,
        check_vma=False,
    )
```

```python
import functools

import jax
import jax.numpy as jnp
from jax import lax
from jax.experimental import pallas as pl
from jax.experimental.pallas import tpu as pltpu
from jax.sharding import PartitionSpec as P

HEAD_DIM = 128
CLUSTERS = 256
WINDOW = 256
SLOTS = 2
NEG_LARGE = -1e30
EMPTY_KEY = 64.0
MESH = pl.DeviceIdType.MESH
SCALE = HEAD_DIM**-0.5
F32 = jnp.float32
BF16 = jnp.bfloat16


def nt(a, b):
    return lax.dot_general(a, b, (((1,), (1,)), ((), ())), preferred_element_type=F32)


def tn(a, b):
    return lax.dot_general(a, b, (((0,), (0,)), ((), ())), preferred_element_type=F32)


def nn(a, b):
    return jnp.dot(a, b, preferred_element_type=F32)


def attend(query, key, value, grad, allowed):
    scores = jnp.where(allowed, nt(query, key) * SCALE, NEG_LARGE)
    top = jnp.max(scores, axis=-1, keepdims=True)
    exps = jnp.where(allowed, jnp.exp(scores - top), 0.0)
    total = jnp.maximum(jnp.sum(exps, axis=-1, keepdims=True), 1.0)
    weights = exps * (1.0 / total)
    weights16 = weights.astype(BF16)
    attended = nn(weights16, value)
    row_dot = jnp.sum(grad.astype(F32) * attended, axis=-1, keepdims=True)
    grad_scores = (weights16.astype(F32) * (nt(grad, value) - row_dot)).astype(BF16)
    grad_query = nn(grad_scores, key) * SCALE
    grad_key = tn(grad_scores, query) * SCALE
    grad_value = tn(weights16, grad)
    return attended, grad_query, grad_key, grad_value


def wide_kernel(
    owners, peers, heads, rows,
    q_ref, k_ref, v_ref, g_ref, ids_ref,
    out_o, out_q, out_k, out_v,
    sbuf, rbuf, bsend, brecv, halo, hsend, hrecv, win, idr, crow, ccol, tcol,
    id_sem, halo_sem, hback_sem, send_sem, recv_sem, bsend_sem, brecv_sem,
):
    me = lax.axis_index("ctx")
    my_head = lax.axis_index("head")
    nxt = lax.rem(me + 1, owners)
    prv = lax.rem(me + owners - 1, owners)
    pairs = heads // 2
    each = CLUSTERS // owners
    slot_rows = owners * SLOTS * 2 * each
    pair_rows = 2 * rows

    barrier = pltpu.get_barrier_semaphore()

    def greet(i, c):
        pl.semaphore_signal(barrier, inc=1, device_id={"ctx": lax.rem(me + i, owners)}, device_id_type=MESH)
        return c

    lax.fori_loop(1, owners, greet, 0)
    for i in range(1, peers):
        pl.semaphore_signal(barrier, inc=1, device_id={"head": lax.rem(my_head + i, peers)}, device_id_type=MESH)
    pl.semaphore_wait(barrier, owners - 1 + peers - 1)

    id_copies = []
    for i in range(1, peers):
        peer = lax.rem(my_head + i, peers)
        copy = pltpu.make_async_remote_copy(
            src_ref=ids_ref.at[peer], dst_ref=idr.at[i - 1],
            send_sem=id_sem.at[0, i - 1], recv_sem=id_sem.at[1, i - 1],
            device_id={"head": peer}, device_id_type=MESH,
        )
        copy.start()
        id_copies.append(copy)
    halo_copies = []
    for i, ref in enumerate((k_ref, v_ref)):
        copy = pltpu.make_async_remote_copy(
            src_ref=ref, dst_ref=halo.at[i], send_sem=halo_sem.at[0, i], recv_sem=halo_sem.at[1, i],
            device_id={"ctx": nxt}, device_id_type=MESH,
        )
        copy.start()
        halo_copies.append(copy)
    for copy in id_copies:
        copy.wait()
    ids = ids_ref[my_head]
    for i in range(1, peers):
        ids = ids + idr[i - 1]
    head_row = lax.broadcasted_iota(jnp.int32, (heads, rows), 0)
    spot = (ids * (1 + 36 * head_row)) & (CLUSTERS - 1)
    eye = (
        lax.broadcasted_iota(jnp.int32, (rows, rows), 0) == lax.broadcasted_iota(jnp.int32, (rows, rows), 1)
    ).astype(BF16)
    spot_t = nt(eye, spot.astype(F32).astype(BF16)).astype(jnp.int32)
    for h in range(heads):
        crow[h] = spot[h : h + 1, :]
        ccol[h] = spot_t[:, h : h + 1]

    sub_tok = lax.broadcasted_iota(jnp.int32, (rows, rows), 0)
    lane_tok = lax.broadcasted_iota(jnp.int32, (rows, rows), 1)

    def place(spots, rank, hh):
        return (spots // each) * (SLOTS * 2 * each) + rank * (2 * each) + hh * each + spots % each

    def columns(h):
        return pl.ds(pl.multiple_of(h * HEAD_DIM, HEAD_DIM), HEAD_DIM)

    def build(p, c):
        lanes, tokens = [], []
        for hh in range(2):
            h = 2 * p + hh
            row, col = crow[h], ccol[h]
            same = col == row
            rank_row = jnp.sum(jnp.where(same & (sub_tok < lane_tok), 1.0, 0.0), axis=0, keepdims=True)
            rank_col = jnp.sum(jnp.where(same & (lane_tok < sub_tok), 1.0, 0.0), axis=1, keepdims=True)
            lanes.append(place(row, rank_row.astype(jnp.int32), hh))
            tcol[h] = place(col, rank_col.astype(jnp.int32), hh)
            tokens.append(jnp.concatenate([r[:, columns(h)] for r in (q_ref, k_ref, v_ref, g_ref)], axis=1))
        lane = jnp.concatenate(lanes, axis=1)
        token = jnp.concatenate(tokens, axis=0)
        hit = lax.broadcasted_iota(jnp.int32, (slot_rows, pair_rows), 0) == lane
        one_hot = jnp.where(hit, 1.0, 0.0)
        empty = jnp.where(jnp.sum(one_hot, axis=1, keepdims=True) > 0.5, 0.0, EMPTY_KEY)
        filled = nn(one_hot.astype(BF16), token)
        key_lane = lax.broadcasted_iota(jnp.int32, (1, 4 * HEAD_DIM), 1)
        mark = jnp.where((key_lane >= HEAD_DIM) & (key_lane < 2 * HEAD_DIM), 1.0, 0.0)
        filled = filled + empty * mark
        sbuf[p] = filled.astype(BF16).reshape(owners, SLOTS, 2 * each, 4 * HEAD_DIM)

        def send(i, c):
            dst = lax.rem(me + i, owners)
            pltpu.make_async_remote_copy(
                src_ref=sbuf.at[p, dst], dst_ref=rbuf.at[p, me], send_sem=send_sem.at[p], recv_sem=recv_sem.at[p],
                device_id={"ctx": dst}, device_id_type=MESH,
            ).start()
            return c

        lax.fori_loop(1, owners, send, 0)
        pltpu.make_async_copy(sbuf.at[p, me], rbuf.at[p, me], recv_sem.at[p]).start()
        return c

    lax.fori_loop(0, pairs, build, 0)

    for copy in halo_copies:
        copy.wait()
    q_pos = lax.broadcasted_iota(jnp.int32, (rows, WINDOW + rows), 0)
    k_pos = lax.broadcasted_iota(jnp.int32, (rows, WINDOW + rows), 1) - WINDOW
    in_window = (k_pos <= q_pos) & (k_pos > q_pos - WINDOW) & (k_pos + me * rows >= 0)

    def window(h, c):
        cols = columns(h)
        key_all = jnp.concatenate([halo[0, :, cols], k_ref[:, cols]], axis=0)
        value_all = jnp.concatenate([halo[1, :, cols], v_ref[:, cols]], axis=0)
        att, gq, gk, gv = attend(q_ref[:, cols], key_all, value_all, g_ref[:, cols], in_window)
        win[0, :, cols] = att
        win[1, :, cols] = gq
        win[2, :, cols] = gk[WINDOW:]
        win[3, :, cols] = gv[WINDOW:]
        hsend[0, :, cols] = gk[:WINDOW].astype(BF16)
        hsend[1, :, cols] = gv[:WINDOW].astype(BF16)
        return c

    lax.fori_loop(0, heads, window, 0)
    back_copies = []
    for i in range(2):
        copy = pltpu.make_async_remote_copy(
            src_ref=hsend.at[i], dst_ref=hrecv.at[i], send_sem=hback_sem.at[0, i], recv_sem=hback_sem.at[1, i],
            device_id={"ctx": prv}, device_id_type=MESH,
        )
        copy.start()
        back_copies.append(copy)

    groups = 2 * each
    part = owners * groups
    p_row = lax.broadcasted_iota(jnp.int32, (part, part), 0)
    p_col = lax.broadcasted_iota(jnp.int32, (part, part), 1)
    to_group = jnp.where(p_col == (p_row % owners) * groups + p_row // owners, 1.0, 0.0).astype(BF16)
    from_group = jnp.where(p_col == (p_row % groups) * owners + p_row // groups, 1.0, 0.0).astype(BF16)
    capacity = owners * SLOTS
    a_pos = lax.broadcasted_iota(jnp.int32, (capacity, capacity), 0)
    b_pos = lax.broadcasted_iota(jnp.int32, (capacity, capacity), 1)
    causal = (b_pos % owners) * SLOTS + b_pos // owners <= (a_pos % owners) * SLOTS + a_pos // owners
    first = jnp.where(lax.broadcasted_iota(jnp.int32, (8, HEAD_DIM), 1) == 0, 1.0, 0.0).astype(BF16)

    def cluster(p, c):
        pltpu.make_async_copy(rbuf.at[p], rbuf.at[p], recv_sem.at[p]).wait()
        slots = [
            nn(to_group, rbuf[p, :, r].reshape(part, 4 * HEAD_DIM)).astype(BF16) for r in range(SLOTS)
        ]
        results = [[], []]
        for g in range(groups):
            packed = jnp.concatenate([s[g * owners : (g + 1) * owners] for s in slots], axis=0)
            query, key, value, grad = (packed[:, i * HEAD_DIM : (i + 1) * HEAD_DIM] for i in range(4))
            valid = nt(first, key)[0:1, :] < EMPTY_KEY / 2
            done = attend(query, key, value, grad, causal & valid)
            done = jnp.concatenate([d.astype(BF16) for d in done], axis=1)
            for r in range(SLOTS):
                results[r].append(done[r * owners : (r + 1) * owners])
        for r in range(SLOTS):
            back = nn(from_group, jnp.concatenate(results[r], axis=0)).astype(BF16)
            bsend[p, :, r] = back.reshape(owners, groups, 4 * HEAD_DIM)

        def send(i, c):
            dst = lax.rem(me + i, owners)
            pltpu.make_async_remote_copy(
                src_ref=bsend.at[p, dst], dst_ref=brecv.at[p, me], send_sem=bsend_sem.at[p],
                recv_sem=brecv_sem.at[p], device_id={"ctx": dst}, device_id_type=MESH,
            ).start()
            return c

        lax.fori_loop(1, owners, send, 0)
        pltpu.make_async_copy(bsend.at[p, me], brecv.at[p, me], brecv_sem.at[p]).start()
        return c

    lax.fori_loop(0, pairs, cluster, 0)

    for copy in back_copies:
        copy.wait()

    def finish(p, c):
        pltpu.make_async_copy(brecv.at[p], brecv.at[p], brecv_sem.at[p]).wait()
        target = jnp.concatenate([tcol[2 * p], tcol[2 * p + 1]], axis=0)
        hit = lax.broadcasted_iota(jnp.int32, (pair_rows, slot_rows), 1) == target
        mine = nn(jnp.where(hit, 1.0, 0.0).astype(BF16), brecv[p].reshape(slot_rows, 4 * HEAD_DIM))
        for hh in range(2):
            cols = columns(2 * p + hh)
            part_of = [mine[hh * rows : (hh + 1) * rows, i * HEAD_DIM : (i + 1) * HEAD_DIM] for i in range(4)]
            out_o[:, cols] = (win[0, :, cols] + part_of[0]).astype(BF16)
            out_q[:, cols] = (win[1, :, cols] + part_of[1]).astype(BF16)
            out_k[:, cols] = (win[2, :, cols] + hrecv[0, :, cols].astype(F32) + part_of[2]).astype(BF16)
            out_v[:, cols] = (win[3, :, cols] + hrecv[1, :, cols].astype(F32) + part_of[3]).astype(BF16)
        return c

    lax.fori_loop(0, pairs, finish, 0)

    def drain(p, c):
        pltpu.make_async_copy(sbuf.at[p, pl.ds(0, owners - 1)], sbuf.at[p, pl.ds(0, owners - 1)], send_sem.at[p]).wait()
        pltpu.make_async_copy(bsend.at[p, pl.ds(0, owners - 1)], bsend.at[p, pl.ds(0, owners - 1)], bsend_sem.at[p]).wait()
        return c

    lax.fori_loop(0, pairs, drain, 0)


TABLE = (1, 37, 91, 151, 203, 117, 173, 55)
LINE = 8
FIRST_CAP = 48
NEXT_CAP = 80
META = 128


def kernel(
    owners, peers, heads, rows,
    q_ref, k_ref, v_ref, g_ref, ids_ref,
    out_o, out_q, out_k, out_v, out_flag,
    sbuf, rbuf, bsend, brecv, halo, hsend, hrecv, win, idr, crow, ccol, trow, tcol, erow, ecol,
    acc, e1, r1, e2, r2, back_acc, e3, r3, e4, r4, relay_row, expand_row, flag_out, flag_y, flag_in,
    id_sem, halo_sem, hback_sem, send_sem, recv_sem, bsend_sem, brecv_sem, e_send, e_recv, fy_sem, f_send, f_recv,
):
    me = lax.axis_index("ctx")
    my_head = lax.axis_index("head")
    nxt = lax.rem(me + 1, owners)
    prv = lax.rem(me + owners - 1, owners)
    my_x, my_z, my_c = me // 16, (me // 2) % LINE, me % 2
    my_w = my_x * 2 + my_c
    pairs = heads // 2
    each = CLUSTERS // owners
    groups = 2 * each
    part = owners * groups
    pair_rows = 2 * rows
    wide = 4 * HEAD_DIM
    first_rows, next_rows = LINE * FIRST_CAP, LINE * NEXT_CAP

    barrier = pltpu.get_barrier_semaphore()

    def greet(i, c):
        pl.semaphore_signal(barrier, inc=1, device_id={"ctx": lax.rem(me + i, owners)}, device_id_type=MESH)
        return c

    lax.fori_loop(1, owners, greet, 0)
    for i in range(1, peers):
        pl.semaphore_signal(barrier, inc=1, device_id={"head": lax.rem(my_head + i, peers)}, device_id_type=MESH)
    pl.semaphore_wait(barrier, owners - 1 + peers - 1)

    id_copies = []
    for i in range(1, peers):
        peer = lax.rem(my_head + i, peers)
        copy = pltpu.make_async_remote_copy(
            src_ref=ids_ref.at[peer], dst_ref=idr.at[i - 1],
            send_sem=id_sem.at[0, i - 1], recv_sem=id_sem.at[1, i - 1],
            device_id={"head": peer}, device_id_type=MESH,
        )
        copy.start()
        id_copies.append(copy)
    sub_tok = lax.broadcasted_iota(jnp.int32, (rows, rows), 0)
    lane_tok = lax.broadcasted_iota(jnp.int32, (rows, rows), 1)
    eye = jnp.where(sub_tok == lane_tok, 1.0, 0.0).astype(BF16)
    before = jnp.where(sub_tok < lane_tok, 1.0, 0.0).astype(BF16)
    head_row = lax.broadcasted_iota(jnp.int32, (heads, rows), 0)
    factor = jnp.zeros((heads, rows), jnp.int32)
    for h in range(heads):
        factor = jnp.where(head_row == h, TABLE[h % 8], factor)
    for copy in id_copies:
        copy.wait()
    ids = ids_ref[my_head]
    for i in range(1, peers):
        ids = ids + idr[i - 1]
    spot = (ids * factor + 29 * head_row) & (CLUSTERS - 1)
    spot_t = nt(eye, spot.astype(F32).astype(BF16)).astype(jnp.int32)
    for h in range(heads):
        crow[h] = spot[h : h + 1, :]
        ccol[h] = spot_t[:, h : h + 1]

    def columns(h):
        return pl.ds(pl.multiple_of(h * HEAD_DIM, HEAD_DIM), HEAD_DIM)

    def tokens_of(h):
        return jnp.concatenate([r[:, columns(h)] for r in (q_ref, k_ref, v_ref, g_ref)], axis=1)

    def line_of(spots):
        return (spots // each // 2) % LINE

    line_row = lax.broadcasted_iota(jnp.int32, (LINE, rows), 0)

    def rank(h, used):
        row, col = crow[h], ccol[h]
        same = col == row
        rank_row = jnp.sum(jnp.where(same & (sub_tok < lane_tok), 1.0, 0.0), axis=0, keepdims=True)
        rank_col = jnp.sum(jnp.where(same & (lane_tok < sub_tok), 1.0, 0.0), axis=1, keepdims=True)
        base = (h % 2) * each
        trow[h] = jnp.where(rank_row < 0.5, row // each * groups + base + row % each, -1)
        tcol[h] = jnp.where(rank_col < 0.5, col // each * groups + base + col % each, -1)
        chosen = jnp.where((line_row == line_of(row)) & (rank_row > 0.5), 1.0, 0.0)
        ahead = nn(chosen.astype(BF16), before) + used
        spot_in = jnp.sum(chosen * ahead, axis=0, keepdims=True)
        spot_in = jnp.where(rank_row > 0.5, jnp.minimum(spot_in, 250.0), 250.0)
        erow[h] = spot_in.astype(jnp.int32)
        spot_col = nt(eye, jnp.broadcast_to(spot_in, (8, rows)).astype(BF16))[:, 0:1].astype(jnp.int32)
        ecol[h] = jnp.where(spot_col < FIRST_CAP, line_of(col) * FIRST_CAP + spot_col, -1)
        return used + jnp.sum(chosen, axis=1, keepdims=True)

    used = lax.fori_loop(0, heads, rank, jnp.zeros((LINE, 1), F32))
    spill = jnp.max(used, axis=0, keepdims=True) - FIRST_CAP

    lane_wide = lax.broadcasted_iota(jnp.int32, (1, wide), 1)
    key_mark = jnp.where((lane_wide >= HEAD_DIM) & (lane_wide < 2 * HEAD_DIM), 1.0, 0.0)

    def build(p, c):
        lane = jnp.concatenate([trow[2 * p], trow[2 * p + 1]], axis=1)
        token = jnp.concatenate([tokens_of(2 * p), tokens_of(2 * p + 1)], axis=0)
        one_hot = jnp.where(lax.broadcasted_iota(jnp.int32, (part, pair_rows), 0) == lane, 1.0, 0.0)
        empty = jnp.where(jnp.sum(one_hot, axis=1, keepdims=True) > 0.5, 0.0, EMPTY_KEY)
        filled = nn(one_hot.astype(BF16), token) + empty * key_mark
        sbuf[p] = filled.astype(BF16).reshape(owners, groups, wide)

        def send(i, c):
            dst = lax.rem(me + i, owners)
            pltpu.make_async_remote_copy(
                src_ref=sbuf.at[p, dst], dst_ref=rbuf.at[p, me], send_sem=send_sem.at[p], recv_sem=recv_sem.at[p],
                device_id={"ctx": dst}, device_id_type=MESH,
            ).start()
            return c

        lax.fori_loop(1, owners, send, 0)
        pltpu.make_async_copy(sbuf.at[p, me], rbuf.at[p, me], recv_sem.at[p]).start()
        return c

    def along_z(stage, src, dst):
        def send(i, c):
            z = lax.rem(my_z + i, LINE)
            pltpu.make_async_remote_copy(
                src_ref=src.at[z], dst_ref=dst.at[my_z], send_sem=e_send.at[stage], recv_sem=e_recv.at[stage],
                device_id={"ctx": my_x * 16 + z * 2 + my_c}, device_id_type=MESH,
            ).start()
            return c

        lax.fori_loop(1, LINE, send, 0)
        pltpu.make_async_copy(src.at[my_z], dst.at[my_z], e_recv.at[stage]).start()

    def across(stage, src, dst):
        def send(i, c):
            w = lax.rem(my_w + i, LINE)
            pltpu.make_async_remote_copy(
                src_ref=src.at[w], dst_ref=dst.at[my_w], send_sem=e_send.at[stage], recv_sem=e_recv.at[stage],
                device_id={"ctx": w // 2 * 16 + my_z * 2 + w % 2}, device_id_type=MESH,
            ).start()
            return c

        lax.fori_loop(1, LINE, send, 0)
        pltpu.make_async_copy(src.at[my_w], dst.at[my_w], e_recv.at[stage]).start()

    def arrived(stage, dst):
        pltpu.make_async_copy(dst, dst, e_recv.at[stage]).wait()

    build(0, 0)

    lane_meta = lax.broadcasted_iota(jnp.int32, (rows, META), 1)
    acc[...] = jnp.zeros_like(acc)

    def second(h, c):
        place = erow[h]
        target = jnp.where(place < FIRST_CAP, line_of(crow[h]) * FIRST_CAP + place, -1)
        one_hot = jnp.where(lax.broadcasted_iota(jnp.int32, (first_rows, rows), 0) == target, 1.0, 0.0).astype(BF16)
        meta = jnp.where(lane_meta == 0, ccol[h], jnp.where(lane_meta == 1, h, jnp.where(lane_meta == 2, me, 1)))
        meta = jnp.where(lane_meta < 4, meta, 0).astype(F32).astype(BF16)
        acc[...] += nn(one_hot, jnp.concatenate([tokens_of(h), meta], axis=1))
        return c

    lax.fori_loop(0, heads, second, 0)
    e1[...] = acc[...].astype(BF16).reshape(LINE, FIRST_CAP, wide + META)
    along_z(0, e1, r1)

    build(1, 0)
    halo_copies = []
    for i, ref in enumerate((k_ref, v_ref)):
        copy = pltpu.make_async_remote_copy(
            src_ref=ref, dst_ref=halo.at[i], send_sem=halo_sem.at[0, i], recv_sem=halo_sem.at[1, i],
            device_id={"ctx": nxt}, device_id_type=MESH,
        )
        copy.start()
        halo_copies.append(copy)
    lax.fori_loop(2, pairs, build, 0)

    arrived(0, r1)
    pick = jnp.where(
        lax.broadcasted_iota(jnp.int32, (8, META), 0) == lax.broadcasted_iota(jnp.int32, (8, META), 1), 1.0, 0.0
    ).astype(BF16)
    came = r1[...].reshape(first_rows, wide + META)
    labels = nt(pick, came[:, wide:])
    owner = labels[0:1].astype(jnp.int32) // each
    live = labels[3:4] > 0.5
    across_row = lax.broadcasted_iota(jnp.int32, (LINE, first_rows), 0)
    chosen = jnp.where((across_row == owner // 16 * 2 + owner % 2) & live, 1.0, 0.0)
    earlier = jnp.where(
        lax.broadcasted_iota(jnp.int32, (first_rows, first_rows), 0)
        < lax.broadcasted_iota(jnp.int32, (first_rows, first_rows), 1), 1.0, 0.0,
    ).astype(BF16)
    place = jnp.sum(chosen * nn(chosen.astype(BF16), earlier), axis=0, keepdims=True).astype(jnp.int32)
    target = jnp.where(live & (place < NEXT_CAP), (owner // 16 * 2 + owner % 2) * NEXT_CAP + place, -1)
    relay_row[...] = target
    count = jnp.max(jnp.sum(chosen, axis=1, keepdims=True), axis=0, keepdims=True)
    spill = jnp.maximum(spill, count - NEXT_CAP)
    flag_out[0] = jnp.broadcast_to(jnp.where(spill > 0.5, 1.0, 0.0), (1, META))

    def relay_hot():
        hit = lax.broadcasted_iota(jnp.int32, (next_rows, first_rows), 0) == relay_row[...]
        return jnp.where(hit, 1.0, 0.0).astype(BF16)

    e2[...] = nn(relay_hot(), came).astype(BF16).reshape(LINE, NEXT_CAP, wide + META)
    across(1, e2, r2)

    for copy in halo_copies:
        copy.wait()
    q_pos = lax.broadcasted_iota(jnp.int32, (rows, WINDOW + rows), 0)
    k_pos = lax.broadcasted_iota(jnp.int32, (rows, WINDOW + rows), 1) - WINDOW
    in_window = (k_pos <= q_pos) & (k_pos > q_pos - WINDOW) & (k_pos + me * rows >= 0)

    def window(h, c):
        cols = columns(h)
        key_all = jnp.concatenate([halo[0, :, cols], k_ref[:, cols]], axis=0)
        value_all = jnp.concatenate([halo[1, :, cols], v_ref[:, cols]], axis=0)
        att, gq, gk, gv = attend(q_ref[:, cols], key_all, value_all, g_ref[:, cols], in_window)
        win[0, :, cols] = att
        win[1, :, cols] = gq
        win[2, :, cols] = gk[WINDOW:]
        win[3, :, cols] = gv[WINDOW:]
        hsend[0, :, cols] = gk[:WINDOW].astype(BF16)
        hsend[1, :, cols] = gv[:WINDOW].astype(BF16)
        return c

    lax.fori_loop(0, heads, window, 0)
    back_copies = []
    for i in range(2):
        copy = pltpu.make_async_remote_copy(
            src_ref=hsend.at[i], dst_ref=hrecv.at[i], send_sem=hback_sem.at[0, i], recv_sem=hback_sem.at[1, i],
            device_id={"ctx": prv}, device_id_type=MESH,
        )
        copy.start()
        back_copies.append(copy)

    flag_copies = []
    for i in range(1, peers):
        copy = pltpu.make_async_remote_copy(
            src_ref=flag_out.at[0], dst_ref=flag_y.at[i - 1], send_sem=fy_sem.at[0, i - 1],
            recv_sem=fy_sem.at[1, i - 1], device_id={"head": lax.rem(my_head + i, peers)}, device_id_type=MESH,
        )
        copy.start()
        flag_copies.append(copy)
    for copy in flag_copies:
        copy.wait()
    raised = flag_out[0]
    for i in range(1, peers):
        raised = jnp.maximum(raised, flag_y[i - 1])
    flag_out[1] = raised

    arrived(1, r2)
    guests = r2[...].reshape(next_rows, wide + META)
    labels = nt(pick, guests[:, wide:]).astype(jnp.int32)
    spots, whose, block, live = labels[0:1], labels[1:2], labels[2:3], labels[3:4]
    for p in range(pairs):
        seat = ((whose % 2) * each + spots % each) * owners + block
        expand_row[p] = jnp.where((live > 0) & (whose // 2 == p), seat, -1)
    p_row = lax.broadcasted_iota(jnp.int32, (part, part), 0)
    p_col = lax.broadcasted_iota(jnp.int32, (part, part), 1)
    to_group = jnp.where(p_col == (p_row % owners) * groups + p_row // owners, 1.0, 0.0).astype(BF16)
    from_group = jnp.where(p_col == (p_row % groups) * owners + p_row // groups, 1.0, 0.0).astype(BF16)
    capacity = owners * SLOTS
    a_pos = lax.broadcasted_iota(jnp.int32, (capacity, capacity), 0)
    b_pos = lax.broadcasted_iota(jnp.int32, (capacity, capacity), 1)
    causal = (b_pos % owners) * SLOTS + b_pos // owners <= (a_pos % owners) * SLOTS + a_pos // owners
    first = jnp.where(lax.broadcasted_iota(jnp.int32, (8, HEAD_DIM), 1) == 0, 1.0, 0.0).astype(BF16)
    back_acc[...] = jnp.zeros_like(back_acc)

    def cluster(p, c):
        pltpu.make_async_copy(rbuf.at[p], rbuf.at[p], recv_sem.at[p]).wait()
        hit = lax.broadcasted_iota(jnp.int32, (part, next_rows), 0) == expand_row[p]
        seats = jnp.where(hit, 1.0, 0.0)
        empty = jnp.where(jnp.sum(seats, axis=1, keepdims=True) > 0.5, 0.0, EMPTY_KEY)
        seats = seats.astype(BF16)
        guest = r2[...].reshape(next_rows, wide + META)[:, :wide]
        slots = [
            nn(to_group, rbuf[p].reshape(part, wide)).astype(BF16),
            (nn(seats, guest) + empty * key_mark).astype(BF16),
        ]
        results = [[], []]
        for g in range(groups):
            packed = jnp.concatenate([s[g * owners : (g + 1) * owners] for s in slots], axis=0)
            query, key, value, grad = (packed[:, i * HEAD_DIM : (i + 1) * HEAD_DIM] for i in range(4))
            valid = nt(first, key)[0:1, :] < EMPTY_KEY / 2
            done = attend(query, key, value, grad, causal & valid)
            done = jnp.concatenate([d.astype(BF16) for d in done], axis=1)
            for r in range(SLOTS):
                results[r].append(done[r * owners : (r + 1) * owners])
        back = nn(from_group, jnp.concatenate(results[0], axis=0)).astype(BF16)
        bsend[p] = back.reshape(owners, groups, wide)

        def send(i, c):
            dst = lax.rem(me + i, owners)
            pltpu.make_async_remote_copy(
                src_ref=bsend.at[p, dst], dst_ref=brecv.at[p, me], send_sem=bsend_sem.at[p],
                recv_sem=brecv_sem.at[p], device_id={"ctx": dst}, device_id_type=MESH,
            ).start()
            return c

        lax.fori_loop(1, owners, send, 0)
        pltpu.make_async_copy(bsend.at[p, me], brecv.at[p, me], brecv_sem.at[p]).start()
        back_acc[...] += tn(seats, jnp.concatenate(results[1], axis=0))
        return c

    lax.fori_loop(0, pairs, cluster, 0)
    e3[...] = back_acc[...].astype(BF16).reshape(LINE, NEXT_CAP, wide)
    across(2, e3, r3)

    def tell(i, c):
        dst = lax.rem(me + i, owners)
        pltpu.make_async_remote_copy(
            src_ref=flag_out.at[1], dst_ref=flag_in.at[me], send_sem=f_send, recv_sem=f_recv,
            device_id={"ctx": dst}, device_id_type=MESH,
        ).start()
        return c

    lax.fori_loop(1, owners, tell, 0)
    pltpu.make_async_copy(flag_out.at[1], flag_in.at[me], f_recv).start()

    arrived(2, r3)
    e4[...] = tn(relay_hot(), r3[...].reshape(next_rows, wide)).astype(BF16).reshape(LINE, FIRST_CAP, wide)
    along_z(3, e4, r4)

    for copy in back_copies:
        copy.wait()

    def settle(p, c):
        pltpu.make_async_copy(brecv.at[p], brecv.at[p], brecv_sem.at[p]).wait()
        target = jnp.concatenate([tcol[2 * p], tcol[2 * p + 1]], axis=0)
        hit = lax.broadcasted_iota(jnp.int32, (pair_rows, part), 1) == target
        mine = nn(jnp.where(hit, 1.0, 0.0).astype(BF16), brecv[p].reshape(part, wide))
        for hh in range(2):
            cols = columns(2 * p + hh)
            for i in range(4):
                both = win[i, :, cols] + mine[hh * rows : (hh + 1) * rows, i * HEAD_DIM : (i + 1) * HEAD_DIM]
                if i >= 2:
                    both = both + hrecv[i - 2, :, cols].astype(F32)
                win[i, :, cols] = both
        return c

    lax.fori_loop(0, pairs, settle, 0)
    arrived(3, r4)

    def finish(h, c):
        hit = lax.broadcasted_iota(jnp.int32, (rows, first_rows), 1) == ecol[h]
        mine = nn(jnp.where(hit, 1.0, 0.0).astype(BF16), r4[...].reshape(first_rows, wide))
        cols = columns(h)
        for i, out in enumerate((out_o, out_q, out_k, out_v)):
            out[:, cols] = (win[i, :, cols] + mine[:, i * HEAD_DIM : (i + 1) * HEAD_DIM]).astype(BF16)
        return c

    lax.fori_loop(0, heads, finish, 0)
    pltpu.make_async_copy(flag_in, flag_in, f_recv).wait()
    out_flag[...] = jnp.max(flag_in[...], axis=0)

    def drain(p, c):
        some = pl.ds(0, owners - 1)
        pltpu.make_async_copy(sbuf.at[p, some], sbuf.at[p, some], send_sem.at[p]).wait()
        pltpu.make_async_copy(bsend.at[p, some], bsend.at[p, some], bsend_sem.at[p]).wait()
        return c

    lax.fori_loop(0, pairs, drain, 0)
    some = pl.ds(0, LINE - 1)
    for stage, ref in enumerate((e1, e2, e3, e4)):
        pltpu.make_async_copy(ref.at[some], ref.at[some], e_send.at[stage]).wait()
    some = pl.ds(0, owners - 1)
    pltpu.make_async_copy(flag_in.at[some], flag_in.at[some], f_send).wait()


def on_device(queries, keys, values, grad_out, cluster_ids):
    rows, width = queries.shape
    heads = width // HEAD_DIM
    owners = lax.axis_size("ctx")
    peers = lax.axis_size("head")
    each = CLUSTERS // owners
    share = rows // peers
    ids = cluster_ids[:, :, 0].reshape(peers, heads, share)
    spread = jnp.zeros((peers, heads, rows), jnp.int32)
    spread = lax.dynamic_update_slice_in_dim(spread, ids, lax.axis_index("head") * share, axis=2)
    pairs = heads // 2
    vmem = pl.BlockSpec(memory_space=pltpu.VMEM)
    dma = pltpu.SemaphoreType.DMA
    args = (queries, keys, values, grad_out, spread)
    result = jax.ShapeDtypeStruct((rows, width), BF16)
    wide = 4 * HEAD_DIM

    def call(body, outs, scratch, number):
        return pl.pallas_call(
            functools.partial(body, owners, peers, heads, rows),
            out_shape=outs,
            in_specs=[vmem] * 5,
            out_specs=[vmem] * len(outs),
            scratch_shapes=scratch,
            compiler_params=pltpu.CompilerParams(
                collective_id=number, has_side_effects=True, vmem_limit_bytes=60 * 1024 * 1024
            ),
        )(*args)

    buffer = pltpu.VMEM((pairs, owners, SLOTS, 2 * each, wide), BF16)
    narrow = pltpu.VMEM((pairs, owners, 2 * each, wide), BF16)
    window = [pltpu.VMEM((2, WINDOW, width), BF16)] * 3 + [pltpu.VMEM((4, rows, width), F32)]
    row_list = pltpu.VMEM((heads, 1, rows), jnp.int32)
    col_list = pltpu.VMEM((heads, rows, 1), jnp.int32)
    ids_in = pltpu.VMEM((peers - 1, heads, rows), jnp.int32)
    sems = [dma((2, peers - 1)), dma((2, 2)), dma((2, 2)), dma((pairs,)), dma((pairs,)), dma((pairs,)), dma((pairs,))]

    def line(cap, size):
        return pltpu.VMEM((LINE, cap, size), BF16)

    *outs, flag = call(
        kernel,
        [result] * 4 + [jax.ShapeDtypeStruct((1, META), F32)],
        [narrow] * 4 + window + [ids_in, row_list, col_list, row_list, col_list, row_list, col_list]
        + [pltpu.VMEM((LINE * FIRST_CAP, wide + META), F32)]
        + [line(FIRST_CAP, wide + META)] * 2 + [line(NEXT_CAP, wide + META)] * 2
        + [pltpu.VMEM((LINE * NEXT_CAP, wide), F32)] + [line(NEXT_CAP, wide)] * 2 + [line(FIRST_CAP, wide)] * 2
        + [pltpu.VMEM((1, LINE * FIRST_CAP), jnp.int32), pltpu.VMEM((pairs, 1, LINE * NEXT_CAP), jnp.int32)]
        + [pltpu.VMEM((2, 1, META), F32), pltpu.VMEM((peers - 1, 1, META), F32), pltpu.VMEM((owners, 1, META), F32)]
        + sems + [dma((4,)), dma((4,)), dma((2, peers - 1)), dma, dma],
        0,
    )

    def again():
        return tuple(call(wide_kernel, [result] * 4, [buffer] * 4 + window + [ids_in, row_list, col_list, col_list] + sems, 1))

    return lax.cond(flag[0, 0] > 0.5, again, lambda: tuple(outs))


def solution(mesh):
    return jax.shard_map(
        on_device,
        mesh=mesh,
        in_specs=(
            P("ctx", "head"), P("ctx", "head"), P("ctx", "head"), P("ctx", "head"),
            P(None, ("ctx", "head"), None),
        ),
        out_specs=(P("ctx", "head"),) * 4,
        check_vma=False,
    )
```

```python
import functools

import jax
import jax.numpy as jnp
from jax import lax
from jax.experimental import pallas as pl
from jax.experimental.pallas import tpu as pltpu
from jax.sharding import PartitionSpec as P

HEAD_DIM = 128
CLUSTERS = 256
WINDOW = 256
SLOTS = 2
NEG_LARGE = -1e30
EMPTY_KEY = 64.0
MESH = pl.DeviceIdType.MESH
SCALE = HEAD_DIM**-0.5
F32 = jnp.float32
BF16 = jnp.bfloat16


def nt(a, b):
    return lax.dot_general(a, b, (((1,), (1,)), ((), ())), preferred_element_type=F32)


def tn(a, b):
    return lax.dot_general(a, b, (((0,), (0,)), ((), ())), preferred_element_type=F32)


def nn(a, b):
    return jnp.dot(a, b, preferred_element_type=F32)


def attend(query, key, value, grad, allowed):
    scores = jnp.where(allowed, nt(query, key) * SCALE, NEG_LARGE)
    top = jnp.max(scores, axis=-1, keepdims=True)
    exps = jnp.where(allowed, jnp.exp(scores - top), 0.0)
    total = jnp.maximum(jnp.sum(exps, axis=-1, keepdims=True), 1.0)
    weights = exps * (1.0 / total)
    weights16 = weights.astype(BF16)
    attended = nn(weights16, value)
    row_dot = jnp.sum(grad.astype(F32) * attended, axis=-1, keepdims=True)
    grad_scores = (weights16.astype(F32) * (nt(grad, value) - row_dot)).astype(BF16)
    grad_query = nn(grad_scores, key) * SCALE
    grad_key = tn(grad_scores, query) * SCALE
    grad_value = tn(weights16, grad)
    return attended, grad_query, grad_key, grad_value


def attend_groups(packed, allowed):
    size = packed[0].shape[0]
    query, key, value, grad = (
        [one[:, i * HEAD_DIM : (i + 1) * HEAD_DIM] for one in packed] for i in range(4)
    )

    def each(product, left, right):
        return jnp.concatenate([product(a, b) for a, b in zip(left, right)], axis=0)

    def split(rows):
        return [rows[i * size : (i + 1) * size] for i in range(len(packed))]

    scores = jnp.where(allowed, each(nt, query, key) * SCALE, NEG_LARGE)
    top = jnp.max(scores, axis=-1, keepdims=True)
    exps = jnp.where(allowed, jnp.exp(scores - top), 0.0)
    total = jnp.maximum(jnp.sum(exps, axis=-1, keepdims=True), 1.0)
    weights16 = (exps * (1.0 / total)).astype(BF16)
    parts = split(weights16)
    attended = each(nn, parts, value)
    row_dot = jnp.sum(jnp.concatenate(grad, axis=0).astype(F32) * attended, axis=-1, keepdims=True)
    grad_scores = (weights16.astype(F32) * (each(nt, grad, value) - row_dot)).astype(BF16)
    changes = split(grad_scores)
    grad_query = each(nn, changes, key) * SCALE
    grad_key = each(tn, changes, query) * SCALE
    grad_value = each(tn, parts, grad)
    done = jnp.concatenate([d.astype(BF16) for d in (attended, grad_query, grad_key, grad_value)], axis=1)
    return split(done)


def wide_kernel(
    owners, peers, heads, rows,
    q_ref, k_ref, v_ref, g_ref, ids_ref,
    out_o, out_q, out_k, out_v,
    sbuf, rbuf, bsend, brecv, halo, hsend, hrecv, win, idr, crow, ccol, tcol,
    id_sem, halo_sem, hback_sem, send_sem, recv_sem, bsend_sem, brecv_sem,
):
    me = lax.axis_index("ctx")
    my_head = lax.axis_index("head")
    nxt = lax.rem(me + 1, owners)
    prv = lax.rem(me + owners - 1, owners)
    pairs = heads // 2
    each = CLUSTERS // owners
    slot_rows = owners * SLOTS * 2 * each
    pair_rows = 2 * rows

    barrier = pltpu.get_barrier_semaphore()

    def greet(i, c):
        pl.semaphore_signal(barrier, inc=1, device_id={"ctx": lax.rem(me + i, owners)}, device_id_type=MESH)
        return c

    lax.fori_loop(1, owners, greet, 0)
    for i in range(1, peers):
        pl.semaphore_signal(barrier, inc=1, device_id={"head": lax.rem(my_head + i, peers)}, device_id_type=MESH)
    pl.semaphore_wait(barrier, owners - 1 + peers - 1)

    id_copies = []
    for i in range(1, peers):
        peer = lax.rem(my_head + i, peers)
        copy = pltpu.make_async_remote_copy(
            src_ref=ids_ref.at[peer], dst_ref=idr.at[i - 1],
            send_sem=id_sem.at[0, i - 1], recv_sem=id_sem.at[1, i - 1],
            device_id={"head": peer}, device_id_type=MESH,
        )
        copy.start()
        id_copies.append(copy)
    halo_copies = []
    for i, ref in enumerate((k_ref, v_ref)):
        copy = pltpu.make_async_remote_copy(
            src_ref=ref, dst_ref=halo.at[i], send_sem=halo_sem.at[0, i], recv_sem=halo_sem.at[1, i],
            device_id={"ctx": nxt}, device_id_type=MESH,
        )
        copy.start()
        halo_copies.append(copy)
    for copy in id_copies:
        copy.wait()
    ids = ids_ref[my_head]
    for i in range(1, peers):
        ids = ids + idr[i - 1]
    head_row = lax.broadcasted_iota(jnp.int32, (heads, rows), 0)
    spot = (ids * (1 + 36 * head_row)) & (CLUSTERS - 1)
    eye = (
        lax.broadcasted_iota(jnp.int32, (rows, rows), 0) == lax.broadcasted_iota(jnp.int32, (rows, rows), 1)
    ).astype(BF16)
    spot_t = nt(eye, spot.astype(F32).astype(BF16)).astype(jnp.int32)
    for h in range(heads):
        crow[h] = spot[h : h + 1, :]
        ccol[h] = spot_t[:, h : h + 1]

    sub_tok = lax.broadcasted_iota(jnp.int32, (rows, rows), 0)
    lane_tok = lax.broadcasted_iota(jnp.int32, (rows, rows), 1)

    def place(spots, rank, hh):
        return (spots // each) * (SLOTS * 2 * each) + rank * (2 * each) + hh * each + spots % each

    def columns(h):
        return pl.ds(pl.multiple_of(h * HEAD_DIM, HEAD_DIM), HEAD_DIM)

    def build(p, c):
        lanes, tokens = [], []
        for hh in range(2):
            h = 2 * p + hh
            row, col = crow[h], ccol[h]
            same = col == row
            rank_row = jnp.sum(jnp.where(same & (sub_tok < lane_tok), 1.0, 0.0), axis=0, keepdims=True)
            rank_col = jnp.sum(jnp.where(same & (lane_tok < sub_tok), 1.0, 0.0), axis=1, keepdims=True)
            lanes.append(place(row, rank_row.astype(jnp.int32), hh))
            tcol[h] = place(col, rank_col.astype(jnp.int32), hh)
            tokens.append(jnp.concatenate([r[:, columns(h)] for r in (q_ref, k_ref, v_ref, g_ref)], axis=1))
        lane = jnp.concatenate(lanes, axis=1)
        token = jnp.concatenate(tokens, axis=0)
        hit = lax.broadcasted_iota(jnp.int32, (slot_rows, pair_rows), 0) == lane
        one_hot = jnp.where(hit, 1.0, 0.0)
        empty = jnp.where(jnp.sum(one_hot, axis=1, keepdims=True) > 0.5, 0.0, EMPTY_KEY)
        filled = nn(one_hot.astype(BF16), token)
        key_lane = lax.broadcasted_iota(jnp.int32, (1, 4 * HEAD_DIM), 1)
        mark = jnp.where((key_lane >= HEAD_DIM) & (key_lane < 2 * HEAD_DIM), 1.0, 0.0)
        filled = filled + empty * mark
        sbuf[p] = filled.astype(BF16).reshape(owners, SLOTS, 2 * each, 4 * HEAD_DIM)

        def send(i, c):
            dst = lax.rem(me + i, owners)
            pltpu.make_async_remote_copy(
                src_ref=sbuf.at[p, dst], dst_ref=rbuf.at[p, me], send_sem=send_sem.at[p], recv_sem=recv_sem.at[p],
                device_id={"ctx": dst}, device_id_type=MESH,
            ).start()
            return c

        lax.fori_loop(1, owners, send, 0)
        pltpu.make_async_copy(sbuf.at[p, me], rbuf.at[p, me], recv_sem.at[p]).start()
        return c

    lax.fori_loop(0, pairs, build, 0)

    for copy in halo_copies:
        copy.wait()
    q_pos = lax.broadcasted_iota(jnp.int32, (rows, WINDOW + rows), 0)
    k_pos = lax.broadcasted_iota(jnp.int32, (rows, WINDOW + rows), 1) - WINDOW
    in_window = (k_pos <= q_pos) & (k_pos > q_pos - WINDOW) & (k_pos + me * rows >= 0)

    def window(h, c):
        cols = columns(h)
        key_all = jnp.concatenate([halo[0, :, cols], k_ref[:, cols]], axis=0)
        value_all = jnp.concatenate([halo[1, :, cols], v_ref[:, cols]], axis=0)
        att, gq, gk, gv = attend(q_ref[:, cols], key_all, value_all, g_ref[:, cols], in_window)
        win[0, :, cols] = att
        win[1, :, cols] = gq
        win[2, :, cols] = gk[WINDOW:]
        win[3, :, cols] = gv[WINDOW:]
        hsend[0, :, cols] = gk[:WINDOW].astype(BF16)
        hsend[1, :, cols] = gv[:WINDOW].astype(BF16)
        return c

    lax.fori_loop(0, heads, window, 0)
    back_copies = []
    for i in range(2):
        copy = pltpu.make_async_remote_copy(
            src_ref=hsend.at[i], dst_ref=hrecv.at[i], send_sem=hback_sem.at[0, i], recv_sem=hback_sem.at[1, i],
            device_id={"ctx": prv}, device_id_type=MESH,
        )
        copy.start()
        back_copies.append(copy)

    groups = 2 * each
    part = owners * groups
    p_row = lax.broadcasted_iota(jnp.int32, (part, part), 0)
    p_col = lax.broadcasted_iota(jnp.int32, (part, part), 1)
    to_group = jnp.where(p_col == (p_row % owners) * groups + p_row // owners, 1.0, 0.0).astype(BF16)
    from_group = jnp.where(p_col == (p_row % groups) * owners + p_row // groups, 1.0, 0.0).astype(BF16)
    capacity = owners * SLOTS
    a_pos = lax.broadcasted_iota(jnp.int32, (capacity, capacity), 0)
    b_pos = lax.broadcasted_iota(jnp.int32, (capacity, capacity), 1)
    causal = (b_pos % owners) * SLOTS + b_pos // owners <= (a_pos % owners) * SLOTS + a_pos // owners
    first = jnp.where(lax.broadcasted_iota(jnp.int32, (8, HEAD_DIM), 1) == 0, 1.0, 0.0).astype(BF16)

    def cluster(p, c):
        pltpu.make_async_copy(rbuf.at[p], rbuf.at[p], recv_sem.at[p]).wait()
        slots = [
            nn(to_group, rbuf[p, :, r].reshape(part, 4 * HEAD_DIM)).astype(BF16) for r in range(SLOTS)
        ]
        results = [[], []]
        for g in range(groups):
            packed = jnp.concatenate([s[g * owners : (g + 1) * owners] for s in slots], axis=0)
            query, key, value, grad = (packed[:, i * HEAD_DIM : (i + 1) * HEAD_DIM] for i in range(4))
            valid = nt(first, key)[0:1, :] < EMPTY_KEY / 2
            done = attend(query, key, value, grad, causal & valid)
            done = jnp.concatenate([d.astype(BF16) for d in done], axis=1)
            for r in range(SLOTS):
                results[r].append(done[r * owners : (r + 1) * owners])
        for r in range(SLOTS):
            back = nn(from_group, jnp.concatenate(results[r], axis=0)).astype(BF16)
            bsend[p, :, r] = back.reshape(owners, groups, 4 * HEAD_DIM)

        def send(i, c):
            dst = lax.rem(me + i, owners)
            pltpu.make_async_remote_copy(
                src_ref=bsend.at[p, dst], dst_ref=brecv.at[p, me], send_sem=bsend_sem.at[p],
                recv_sem=brecv_sem.at[p], device_id={"ctx": dst}, device_id_type=MESH,
            ).start()
            return c

        lax.fori_loop(1, owners, send, 0)
        pltpu.make_async_copy(bsend.at[p, me], brecv.at[p, me], brecv_sem.at[p]).start()
        return c

    lax.fori_loop(0, pairs, cluster, 0)

    for copy in back_copies:
        copy.wait()

    def finish(p, c):
        pltpu.make_async_copy(brecv.at[p], brecv.at[p], brecv_sem.at[p]).wait()
        target = jnp.concatenate([tcol[2 * p], tcol[2 * p + 1]], axis=0)
        hit = lax.broadcasted_iota(jnp.int32, (pair_rows, slot_rows), 1) == target
        mine = nn(jnp.where(hit, 1.0, 0.0).astype(BF16), brecv[p].reshape(slot_rows, 4 * HEAD_DIM))
        for hh in range(2):
            cols = columns(2 * p + hh)
            part_of = [mine[hh * rows : (hh + 1) * rows, i * HEAD_DIM : (i + 1) * HEAD_DIM] for i in range(4)]
            out_o[:, cols] = (win[0, :, cols] + part_of[0]).astype(BF16)
            out_q[:, cols] = (win[1, :, cols] + part_of[1]).astype(BF16)
            out_k[:, cols] = (win[2, :, cols] + hrecv[0, :, cols].astype(F32) + part_of[2]).astype(BF16)
            out_v[:, cols] = (win[3, :, cols] + hrecv[1, :, cols].astype(F32) + part_of[3]).astype(BF16)
        return c

    lax.fori_loop(0, pairs, finish, 0)

    def drain(p, c):
        pltpu.make_async_copy(sbuf.at[p, pl.ds(0, owners - 1)], sbuf.at[p, pl.ds(0, owners - 1)], send_sem.at[p]).wait()
        pltpu.make_async_copy(bsend.at[p, pl.ds(0, owners - 1)], bsend.at[p, pl.ds(0, owners - 1)], bsend_sem.at[p]).wait()
        return c

    lax.fori_loop(0, pairs, drain, 0)


TABLE = (1, 37, 91, 151, 203, 117, 173, 55)
LINE = 8
FIRST_CAP = 40
NEXT_CAP = 80
META = 128


def kernel(
    owners, peers, heads, rows,
    q_hbm, k_hbm, v_hbm, g_hbm, ids_ref,
    out_o, out_q, out_k, out_v, out_flag,
    q_ref, k_ref, v_ref, g_ref, win, r4, ecol,
    sbuf, rbuf, bsend, brecv, halo, hsend, hrecv, idr, crow, ccol, trow, tcol, erow,
    acc, e1, r1, e2, r2, back_acc, e3, r3, e4, relay_row, expand_row, flag_out, flag_y, flag_in,
    id_sem, halo_sem, hback_sem, send_sem, recv_sem, bsend_sem, brecv_sem, e_send, e_recv, fy_sem, f_send, f_recv, in_sem,
):
    me = lax.axis_index("ctx")
    my_head = lax.axis_index("head")
    nxt = lax.rem(me + 1, owners)
    prv = lax.rem(me + owners - 1, owners)
    my_x, my_z, my_c = me // 16, (me // 2) % LINE, me % 2
    my_w = my_x * 2 + my_c
    pairs = heads // 2
    each = CLUSTERS // owners
    groups = 2 * each
    part = owners * groups
    pair_rows = 2 * rows
    wide = 4 * HEAD_DIM
    first_rows, next_rows = LINE * FIRST_CAP, LINE * NEXT_CAP

    loads = [
        pltpu.make_async_copy(src, dst, in_sem.at[i])
        for i, (src, dst) in enumerate(((k_hbm, k_ref), (v_hbm, v_ref), (q_hbm, q_ref), (g_hbm, g_ref)))
    ]
    for load in loads:
        load.start()
    barrier = pltpu.get_barrier_semaphore()

    def greet(i, c):
        far = lax.rem(i + owners // 2 + 7, owners - 1) + 1
        pl.semaphore_signal(barrier, inc=1, device_id={"ctx": lax.rem(me + far, owners)}, device_id_type=MESH)
        return c

    lax.fori_loop(0, owners - 1, greet, 0)
    for i in range(1, peers):
        pl.semaphore_signal(barrier, inc=1, device_id={"head": lax.rem(my_head + i, peers)}, device_id_type=MESH)
    pl.semaphore_wait(barrier, owners - 1 + peers - 1)

    id_copies = []
    for i in range(1, peers):
        peer = lax.rem(my_head + i, peers)
        copy = pltpu.make_async_remote_copy(
            src_ref=ids_ref.at[peer], dst_ref=idr.at[i - 1],
            send_sem=id_sem.at[0, i - 1], recv_sem=id_sem.at[1, i - 1],
            device_id={"head": peer}, device_id_type=MESH,
        )
        copy.start()
        id_copies.append(copy)
    for load in loads:
        load.wait()
    halo_copies = []
    for i, ref in enumerate((k_ref, v_ref)):
        copy = pltpu.make_async_remote_copy(
            src_ref=ref, dst_ref=halo.at[i], send_sem=halo_sem.at[0, i], recv_sem=halo_sem.at[1, i],
            device_id={"ctx": nxt}, device_id_type=MESH,
        )
        copy.start()
        halo_copies.append(copy)
    sub_tok = lax.broadcasted_iota(jnp.int32, (rows, rows), 0)
    lane_tok = lax.broadcasted_iota(jnp.int32, (rows, rows), 1)
    eye = jnp.where(sub_tok == lane_tok, 1.0, 0.0).astype(BF16)
    before = jnp.where(sub_tok < lane_tok, 1.0, 0.0).astype(BF16)
    head_row = lax.broadcasted_iota(jnp.int32, (heads, rows), 0)
    factor = jnp.zeros((heads, rows), jnp.int32)
    for h in range(heads):
        factor = jnp.where(head_row == h, TABLE[h % 8], factor)
    for copy in id_copies:
        copy.wait()
    ids = ids_ref[my_head]
    for i in range(1, peers):
        ids = ids + idr[i - 1]
    spot = (ids * factor + 29 * head_row) & (CLUSTERS - 1)
    spot_t = nt(eye, spot.astype(F32).astype(BF16)).astype(jnp.int32)
    for h in range(heads):
        crow[h] = spot[h : h + 1, :]
        ccol[h] = spot_t[:, h : h + 1]

    def columns(h):
        return pl.ds(pl.multiple_of(h * HEAD_DIM, HEAD_DIM), HEAD_DIM)

    def tokens_of(h):
        return jnp.concatenate([r[:, columns(h)] for r in (q_ref, k_ref, v_ref, g_ref)], axis=1)

    def line_of(spots):
        return (spots // each // 2) % LINE

    line_row = lax.broadcasted_iota(jnp.int32, (LINE, rows), 0)

    def rank(h, used):
        row, col = crow[h], ccol[h]
        same = col == row
        rank_row = jnp.sum(jnp.where(same & (sub_tok < lane_tok), 1.0, 0.0), axis=0, keepdims=True)
        rank_col = jnp.sum(jnp.where(same & (lane_tok < sub_tok), 1.0, 0.0), axis=1, keepdims=True)
        base = (h % 2) * each
        trow[h] = jnp.where(rank_row < 0.5, row // each * groups + base + row % each, -1)
        tcol[h] = jnp.where(rank_col < 0.5, col // each * groups + base + col % each, -1)
        chosen = jnp.where((line_row == line_of(row)) & (rank_row > 0.5), 1.0, 0.0)
        ahead = nn(chosen.astype(BF16), before) + used
        spot_in = jnp.sum(chosen * ahead, axis=0, keepdims=True)
        spot_in = jnp.where(rank_row > 0.5, jnp.minimum(spot_in, 250.0), 250.0)
        erow[h] = spot_in.astype(jnp.int32)
        spot_col = nt(eye, jnp.broadcast_to(spot_in, (8, rows)).astype(BF16))[:, 0:1].astype(jnp.int32)
        ecol[h] = jnp.where(spot_col < FIRST_CAP, line_of(col) * FIRST_CAP + spot_col, -1)
        return used + jnp.sum(chosen, axis=1, keepdims=True)

    used = lax.fori_loop(0, 2, rank, jnp.zeros((LINE, 1), F32))

    lane_wide = lax.broadcasted_iota(jnp.int32, (1, wide), 1)
    key_mark = jnp.where((lane_wide >= HEAD_DIM) & (lane_wide < 2 * HEAD_DIM), 1.0, 0.0)

    def build(p, c):
        lane = jnp.concatenate([trow[2 * p], trow[2 * p + 1]], axis=1)
        token = jnp.concatenate([tokens_of(2 * p), tokens_of(2 * p + 1)], axis=0)
        one_hot = jnp.where(lax.broadcasted_iota(jnp.int32, (part, pair_rows), 0) == lane, 1.0, 0.0)
        empty = jnp.where(jnp.sum(one_hot, axis=1, keepdims=True) > 0.5, 0.0, EMPTY_KEY)
        filled = nn(one_hot.astype(BF16), token) + empty * key_mark
        sbuf[p] = filled.astype(BF16).reshape(owners, groups, wide)

        def send(i, c):
            dst = lax.rem(me + i, owners)
            pltpu.make_async_remote_copy(
                src_ref=sbuf.at[p, dst], dst_ref=rbuf.at[p, me], send_sem=send_sem.at[p], recv_sem=recv_sem.at[p],
                device_id={"ctx": dst}, device_id_type=MESH,
            ).start()
            return c

        lax.fori_loop(1, owners, send, 0)
        pltpu.make_async_copy(sbuf.at[p, me], rbuf.at[p, me], recv_sem.at[p]).start()
        return c

    def along_z(stage, src, dst):
        def send(i, c):
            z = lax.rem(my_z + i, LINE)
            pltpu.make_async_remote_copy(
                src_ref=src.at[z], dst_ref=dst.at[my_z], send_sem=e_send.at[stage], recv_sem=e_recv.at[stage],
                device_id={"ctx": my_x * 16 + z * 2 + my_c}, device_id_type=MESH,
            ).start()
            return c

        lax.fori_loop(1, LINE, send, 0)
        pltpu.make_async_copy(src.at[my_z], dst.at[my_z], e_recv.at[stage]).start()

    def across(stage, src, dst):
        def send(i, c):
            w = lax.rem(my_w + i, LINE)
            pltpu.make_async_remote_copy(
                src_ref=src.at[w], dst_ref=dst.at[my_w], send_sem=e_send.at[stage], recv_sem=e_recv.at[stage],
                device_id={"ctx": w // 2 * 16 + my_z * 2 + w % 2}, device_id_type=MESH,
            ).start()
            return c

        lax.fori_loop(1, LINE, send, 0)
        pltpu.make_async_copy(src.at[my_w], dst.at[my_w], e_recv.at[stage]).start()

    def arrived(stage, dst):
        pltpu.make_async_copy(dst, dst, e_recv.at[stage]).wait()

    build(0, 0)
    used = lax.fori_loop(2, heads, rank, used)
    spill = jnp.max(used, axis=0, keepdims=True) - FIRST_CAP

    lane_meta = lax.broadcasted_iota(jnp.int32, (rows, META), 1)
    acc[...] = jnp.zeros_like(acc)

    def second(h, c):
        place = erow[h]
        target = jnp.where(place < FIRST_CAP, line_of(crow[h]) * FIRST_CAP + place, -1)
        one_hot = jnp.where(lax.broadcasted_iota(jnp.int32, (first_rows, rows), 0) == target, 1.0, 0.0).astype(BF16)
        meta = jnp.where(lane_meta == 0, ccol[h], jnp.where(lane_meta == 1, h, jnp.where(lane_meta == 2, me, 1)))
        meta = jnp.where(lane_meta < 4, meta, 0).astype(F32).astype(BF16)
        acc[...] += nn(one_hot, jnp.concatenate([tokens_of(h), meta], axis=1))
        return c

    lax.fori_loop(0, heads, second, 0)
    e1[...] = acc[...].astype(BF16).reshape(LINE, FIRST_CAP, wide + META)
    along_z(0, e1, r1)

    build(1, 0)

    for copy in halo_copies:
        copy.wait()
    q_pos = lax.broadcasted_iota(jnp.int32, (rows, WINDOW + rows), 0)
    k_pos = lax.broadcasted_iota(jnp.int32, (rows, WINDOW + rows), 1) - WINDOW
    in_window = (k_pos <= q_pos) & (k_pos > q_pos - WINDOW) & (k_pos + me * rows >= 0)

    def window(h, c):
        cols = columns(h)
        key_all = jnp.concatenate([halo[0, :, cols], k_ref[:, cols]], axis=0)
        value_all = jnp.concatenate([halo[1, :, cols], v_ref[:, cols]], axis=0)
        att, gq, gk, gv = attend(q_ref[:, cols], key_all, value_all, g_ref[:, cols], in_window)
        win[0, :, cols] = att
        win[1, :, cols] = gq
        win[2, :, cols] = gk[WINDOW:]
        win[3, :, cols] = gv[WINDOW:]
        hsend[0, :, cols] = gk[:WINDOW].astype(BF16)
        hsend[1, :, cols] = gv[:WINDOW].astype(BF16)
        return c

    lax.fori_loop(0, heads, window, 0)
    back_copies = []
    for i in range(2):
        copy = pltpu.make_async_remote_copy(
            src_ref=hsend.at[i], dst_ref=hrecv.at[i], send_sem=hback_sem.at[0, i], recv_sem=hback_sem.at[1, i],
            device_id={"ctx": prv}, device_id_type=MESH,
        )
        copy.start()
        back_copies.append(copy)

    lax.fori_loop(2, pairs - 1, build, 0)

    arrived(0, r1)
    pick = jnp.where(
        lax.broadcasted_iota(jnp.int32, (8, META), 0) == lax.broadcasted_iota(jnp.int32, (8, META), 1), 1.0, 0.0
    ).astype(BF16)
    came = r1[...].reshape(first_rows, wide + META)
    labels = nt(pick, came[:, wide:])
    owner = labels[0:1].astype(jnp.int32) // each
    live = labels[3:4] > 0.5
    across_row = lax.broadcasted_iota(jnp.int32, (LINE, first_rows), 0)
    chosen = jnp.where((across_row == owner // 16 * 2 + owner % 2) & live, 1.0, 0.0)
    earlier = jnp.where(
        lax.broadcasted_iota(jnp.int32, (first_rows, first_rows), 0)
        < lax.broadcasted_iota(jnp.int32, (first_rows, first_rows), 1), 1.0, 0.0,
    ).astype(BF16)
    place = jnp.sum(chosen * nn(chosen.astype(BF16), earlier), axis=0, keepdims=True).astype(jnp.int32)
    target = jnp.where(live & (place < NEXT_CAP), (owner // 16 * 2 + owner % 2) * NEXT_CAP + place, -1)
    relay_row[...] = target
    count = jnp.max(jnp.sum(chosen, axis=1, keepdims=True), axis=0, keepdims=True)
    spill = jnp.maximum(spill, count - NEXT_CAP)
    flag_out[0] = jnp.broadcast_to(jnp.where(spill > 0.5, 1.0, 0.0), (1, META))

    def relay_hot():
        hit = lax.broadcasted_iota(jnp.int32, (next_rows, first_rows), 0) == relay_row[...]
        return jnp.where(hit, 1.0, 0.0).astype(BF16)

    e2[...] = nn(relay_hot(), came).astype(BF16).reshape(LINE, NEXT_CAP, wide + META)
    across(1, e2, r2)

    flag_copies = []
    for i in range(1, peers):
        copy = pltpu.make_async_remote_copy(
            src_ref=flag_out.at[0], dst_ref=flag_y.at[i - 1], send_sem=fy_sem.at[0, i - 1],
            recv_sem=fy_sem.at[1, i - 1], device_id={"head": lax.rem(my_head + i, peers)}, device_id_type=MESH,
        )
        copy.start()
        flag_copies.append(copy)
    build(pairs - 1, 0)

    arrived(1, r2)
    guests = r2[...].reshape(next_rows, wide + META)
    labels = nt(pick, guests[:, wide:]).astype(jnp.int32)
    spots, whose, block, live = labels[0:1], labels[1:2], labels[2:3], labels[3:4]
    for p in range(pairs):
        seat = ((whose % 2) * each + spots % each) * owners + block
        expand_row[p] = jnp.where((live > 0) & (whose // 2 == p), seat, -1)
    p_row = lax.broadcasted_iota(jnp.int32, (part, part), 0)
    p_col = lax.broadcasted_iota(jnp.int32, (part, part), 1)
    to_group = jnp.where(p_col == (p_row % owners) * groups + p_row // owners, 1.0, 0.0).astype(BF16)
    from_group = jnp.where(p_col == (p_row % groups) * owners + p_row // groups, 1.0, 0.0).astype(BF16)
    capacity = owners * SLOTS
    a_pos = lax.broadcasted_iota(jnp.int32, (capacity, capacity), 0)
    b_pos = lax.broadcasted_iota(jnp.int32, (capacity, capacity), 1)
    causal = (b_pos % owners) * SLOTS + b_pos // owners <= (a_pos % owners) * SLOTS + a_pos // owners
    first = jnp.where(lax.broadcasted_iota(jnp.int32, (8, HEAD_DIM), 1) == 0, 1.0, 0.0).astype(BF16)
    back_acc[...] = jnp.zeros_like(back_acc)

    def give(p):
        def send(i, c):
            dst = lax.rem(me + i, owners)
            pltpu.make_async_remote_copy(
                src_ref=bsend.at[p, dst], dst_ref=brecv.at[p, me], send_sem=bsend_sem.at[p],
                recv_sem=brecv_sem.at[p], device_id={"ctx": dst}, device_id_type=MESH,
            ).start()
            return c

        lax.fori_loop(1, owners, send, 0)
        pltpu.make_async_copy(bsend.at[p, me], brecv.at[p, me], brecv_sem.at[p]).start()

    def cluster(p, c):
        pltpu.make_async_copy(rbuf.at[p], rbuf.at[p], recv_sem.at[p]).wait()
        hit = lax.broadcasted_iota(jnp.int32, (part, next_rows), 0) == expand_row[p]
        seats = jnp.where(hit, 1.0, 0.0)
        empty = jnp.where(jnp.sum(seats, axis=1, keepdims=True) > 0.5, 0.0, EMPTY_KEY)
        seats = seats.astype(BF16)
        guest = r2[...].reshape(next_rows, wide + META)[:, :wide]
        slots = [
            nn(to_group, rbuf[p].reshape(part, wide)).astype(BF16),
            (nn(seats, guest) + empty * key_mark).astype(BF16),
        ]
        packed = [
            jnp.concatenate([one[g * owners : (g + 1) * owners] for one in slots], axis=0) for g in range(groups)
        ]
        allowed = jnp.concatenate(
            [causal & (nt(first, one[:, HEAD_DIM : 2 * HEAD_DIM])[0:1, :] < EMPTY_KEY / 2) for one in packed], axis=0
        )
        done = attend_groups(packed, allowed)
        results = [[one[r * owners : (r + 1) * owners] for one in done] for r in range(SLOTS)]
        back = nn(from_group, jnp.concatenate(results[0], axis=0)).astype(BF16)
        bsend[p] = back.reshape(owners, groups, wide)
        pl.when(p < pairs - 1)(lambda: give(p))

        back_acc[...] += tn(seats, jnp.concatenate(results[1], axis=0))
        return c

    lax.fori_loop(0, pairs, cluster, 0)
    e3[...] = back_acc[...].astype(BF16).reshape(LINE, NEXT_CAP, wide)
    across(2, e3, r3)
    for copy in flag_copies:
        copy.wait()
    raised = flag_out[0]
    for i in range(1, peers):
        raised = jnp.maximum(raised, flag_y[i - 1])
    flag_out[1] = raised

    def tell(i, c):
        dst = lax.rem(me + i, owners)
        pltpu.make_async_remote_copy(
            src_ref=flag_out.at[1], dst_ref=flag_in.at[me], send_sem=f_send, recv_sem=f_recv,
            device_id={"ctx": dst}, device_id_type=MESH,
        ).start()
        return c

    lax.fori_loop(1, owners, tell, 0)
    pltpu.make_async_copy(flag_out.at[1], flag_in.at[me], f_recv).start()

    arrived(2, r3)
    e4[...] = tn(relay_hot(), r3[...].reshape(next_rows, wide)).astype(BF16).reshape(LINE, FIRST_CAP, wide)
    along_z(3, e4, r4)
    give(pairs - 1)

    for copy in back_copies:
        copy.wait()

    outs = (out_o, out_q, out_k, out_v)

    def settle(p):
        pltpu.make_async_copy(brecv.at[p], brecv.at[p], brecv_sem.at[p]).wait()
        target = jnp.concatenate([tcol[2 * p], tcol[2 * p + 1]], axis=0)
        hit = lax.broadcasted_iota(jnp.int32, (pair_rows, part), 1) == target
        mine = nn(jnp.where(hit, 1.0, 0.0).astype(BF16), brecv[p].reshape(part, wide))
        for hh in range(2):
            cols = columns(2 * p + hh)
            for i in range(4):
                both = win[i, :, cols] + mine[hh * rows : (hh + 1) * rows, i * HEAD_DIM : (i + 1) * HEAD_DIM]
                yield i, cols, both + hrecv[i - 2, :, cols].astype(F32) if i >= 2 else both

    def settle_in(p, c):
        for i, cols, both in settle(p):
            win[i, :, cols] = both
        return c

    lax.fori_loop(0, pairs - 1, settle_in, 0)
    arrived(3, r4)

    def late(h):
        hit = lax.broadcasted_iota(jnp.int32, (rows, first_rows), 1) == ecol[h]
        mine = nn(jnp.where(hit, 1.0, 0.0).astype(BF16), r4[...].reshape(first_rows, wide))
        return [win[i, :, columns(h)] + mine[:, i * HEAD_DIM : (i + 1) * HEAD_DIM] for i in range(4)]

    def late_in(h, c):
        for i, both in enumerate(late(h)):
            win[i, :, columns(h)] = both
        return c

    def late_out(h, c):
        for i, both in enumerate(late(h)):
            outs[i][:, columns(h)] = both.astype(BF16)
        return c

    lax.fori_loop(heads - 2, heads, late_in, 0)
    lax.fori_loop(0, heads - 2, late_out, 0)
    for i, cols, both in settle(pairs - 1):
        outs[i][:, cols] = both.astype(BF16)
    pltpu.make_async_copy(flag_in, flag_in, f_recv).wait()
    out_flag[...] = jnp.max(flag_in[...], axis=0)

    def drain(p, c):
        some = pl.ds(0, owners - 1)
        pltpu.make_async_copy(sbuf.at[p, some], sbuf.at[p, some], send_sem.at[p]).wait()
        pltpu.make_async_copy(bsend.at[p, some], bsend.at[p, some], bsend_sem.at[p]).wait()
        return c

    lax.fori_loop(0, pairs, drain, 0)
    some = pl.ds(0, LINE - 1)
    for stage, ref in enumerate((e1, e2, e3, e4)):
        pltpu.make_async_copy(ref.at[some], ref.at[some], e_send.at[stage]).wait()
    some = pl.ds(0, owners - 1)
    pltpu.make_async_copy(flag_in.at[some], flag_in.at[some], f_send).wait()


def finish_kernel(*refs):
    p = pl.program_id(0)
    for src, out in zip(refs[:4], refs[4:]):
        size = out.shape[0]
        out[...] = src[pl.ds(pl.multiple_of(p * size, size), size), :]


def on_device(queries, keys, values, grad_out, cluster_ids):
    rows, width = queries.shape
    heads = width // HEAD_DIM
    owners = lax.axis_size("ctx")
    peers = lax.axis_size("head")
    each = CLUSTERS // owners
    share = rows // peers
    ids = cluster_ids[:, :, 0].reshape(peers, heads, share)
    spread = jnp.zeros((peers, heads, rows), jnp.int32)
    spread = lax.dynamic_update_slice_in_dim(spread, ids, lax.axis_index("head") * share, axis=2)
    pairs = heads // 2
    vmem = pl.BlockSpec(memory_space=pltpu.VMEM)
    dma = pltpu.SemaphoreType.DMA
    args = (queries, keys, values, grad_out, spread)
    result = jax.ShapeDtypeStruct((rows, width), BF16)
    wide = 4 * HEAD_DIM

    anywhere = pl.BlockSpec(memory_space=pl.ANY)

    def call(body, outs, scratch, number, ins=None, places=None):
        return pl.pallas_call(
            functools.partial(body, owners, peers, heads, rows),
            out_shape=outs,
            in_specs=ins or [vmem] * 5,
            out_specs=places or [vmem] * len(outs),
            scratch_shapes=scratch,
            compiler_params=pltpu.CompilerParams(
                collective_id=number, has_side_effects=True, vmem_limit_bytes=36 * 1024 * 1024
            ),
        )(*args)

    buffer = pltpu.VMEM((pairs, owners, SLOTS, 2 * each, wide), BF16)
    narrow = pltpu.VMEM((pairs, owners, 2 * each, wide), BF16)
    window = [pltpu.VMEM((2, WINDOW, width), BF16)] * 3
    total = pltpu.VMEM((4, rows, width), F32)
    row_list = pltpu.VMEM((heads, 1, rows), jnp.int32)
    col_list = pltpu.VMEM((heads, rows, 1), jnp.int32)
    ids_in = pltpu.VMEM((peers - 1, heads, rows), jnp.int32)
    sems = [dma((2, peers - 1)), dma((2, 2)), dma((2, 2)), dma((pairs,)), dma((pairs,)), dma((pairs,)), dma((pairs,))]

    def line(cap, size):
        return pltpu.VMEM((LINE, cap, size), BF16)

    *outs, flag = call(
        kernel,
        [result] * 4 + [jax.ShapeDtypeStruct((1, META), F32)],
        [pltpu.VMEM((rows, width), BF16)] * 4 + [total, line(FIRST_CAP, wide), col_list] + [narrow] * 4 + window + [ids_in, row_list, col_list, row_list, col_list, row_list]
        + [pltpu.VMEM((LINE * FIRST_CAP, wide + META), F32)]
        + [line(FIRST_CAP, wide + META)] * 2 + [line(NEXT_CAP, wide + META)] * 2
        + [pltpu.VMEM((LINE * NEXT_CAP, wide), F32)] + [line(NEXT_CAP, wide)] * 2 + [line(FIRST_CAP, wide)]
        + [pltpu.VMEM((1, LINE * FIRST_CAP), jnp.int32), pltpu.VMEM((pairs, 1, LINE * NEXT_CAP), jnp.int32)]
        + [pltpu.VMEM((2, 1, META), F32), pltpu.VMEM((peers - 1, 1, META), F32), pltpu.VMEM((owners, 1, META), F32)]
        + sems + [dma((4,)), dma((4,)), dma((2, peers - 1)), dma, dma, dma((4,))],
        0,
        [anywhere] * 4 + [vmem],
        [vmem] * 5,
    )

    def again():
        return tuple(
            call(wide_kernel, [result] * 4, [buffer] * 4 + window + [total, ids_in, row_list, col_list, col_list] + sems, 1)
        )

    outs = lax.cond(flag[0, 0] > 0.5, again, lambda: tuple(outs))
    return pl.pallas_call(
        finish_kernel,
        grid=(pairs,),
        out_shape=[result] * 4,
        in_specs=[vmem] * 4,
        out_specs=[pl.BlockSpec((rows // pairs, width), lambda p: (p, 0))] * 4,
        compiler_params=pltpu.CompilerParams(vmem_limit_bytes=24 * 1024 * 1024),
    )(*outs)


def solution(mesh):
    return jax.shard_map(
        on_device,
        mesh=mesh,
        in_specs=(
            P("ctx", "head"), P("ctx", "head"), P("ctx", "head"), P("ctx", "head"),
            P(None, ("ctx", "head"), None),
        ),
        out_specs=(P("ctx", "head"),) * 4,
        check_vma=False,
    )
```

```python
import functools

import jax
import jax.numpy as jnp
from jax import lax
from jax.experimental import pallas as pl
from jax.experimental.pallas import tpu as pltpu
from jax.sharding import PartitionSpec as P

HEAD_DIM = 128
CLUSTERS = 256
WINDOW = 256
SLOTS = 2
NEG_LARGE = -1e30
EMPTY_KEY = 64.0
MESH = pl.DeviceIdType.MESH
SCALE = HEAD_DIM**-0.5
F32 = jnp.float32
BF16 = jnp.bfloat16


def nt(a, b):
    return lax.dot_general(a, b, (((1,), (1,)), ((), ())), preferred_element_type=F32)


def tn(a, b):
    return lax.dot_general(a, b, (((0,), (0,)), ((), ())), preferred_element_type=F32)


def nn(a, b):
    return jnp.dot(a, b, preferred_element_type=F32)


def attend(query, key, value, grad, allowed):
    scores = jnp.where(allowed, nt(query, key) * SCALE, NEG_LARGE)
    top = jnp.max(scores, axis=-1, keepdims=True)
    exps = jnp.where(allowed, jnp.exp(scores - top), 0.0)
    total = jnp.maximum(jnp.sum(exps, axis=-1, keepdims=True), 1.0)
    weights = exps * (1.0 / total)
    weights16 = weights.astype(BF16)
    attended = nn(weights16, value)
    row_dot = jnp.sum(grad.astype(F32) * attended, axis=-1, keepdims=True)
    grad_scores = (weights16.astype(F32) * (nt(grad, value) - row_dot)).astype(BF16)
    grad_query = nn(grad_scores, key) * SCALE
    grad_key = tn(grad_scores, query) * SCALE
    grad_value = tn(weights16, grad)
    return attended, grad_query, grad_key, grad_value


def attend_groups(packed, allowed):
    size = packed[0].shape[0]
    query, key, value, grad = (
        [one[:, i * HEAD_DIM : (i + 1) * HEAD_DIM] for one in packed] for i in range(4)
    )

    def each(product, left, right):
        return jnp.concatenate([product(a, b) for a, b in zip(left, right)], axis=0)

    def split(rows):
        return [rows[i * size : (i + 1) * size] for i in range(len(packed))]

    scores = jnp.where(allowed, each(nt, query, key) * SCALE, NEG_LARGE)
    top = jnp.max(scores, axis=-1, keepdims=True)
    exps = jnp.where(allowed, jnp.exp(scores - top), 0.0)
    total = jnp.maximum(jnp.sum(exps, axis=-1, keepdims=True), 1.0)
    weights16 = (exps * (1.0 / total)).astype(BF16)
    parts = split(weights16)
    attended = each(nn, parts, value)
    row_dot = jnp.sum(jnp.concatenate(grad, axis=0).astype(F32) * attended, axis=-1, keepdims=True)
    grad_scores = (weights16.astype(F32) * (each(nt, grad, value) - row_dot)).astype(BF16)
    changes = split(grad_scores)
    grad_query = each(nn, changes, key) * SCALE
    grad_key = each(tn, changes, query) * SCALE
    grad_value = each(tn, parts, grad)
    done = jnp.concatenate([d.astype(BF16) for d in (attended, grad_query, grad_key, grad_value)], axis=1)
    return split(done)


def wide_kernel(
    owners, peers, heads, rows,
    q_ref, k_ref, v_ref, g_ref, ids_ref,
    out_o, out_q, out_k, out_v,
    sbuf, rbuf, bsend, brecv, halo, hsend, hrecv, win, idr, crow, ccol, tcol,
    id_sem, halo_sem, hback_sem, send_sem, recv_sem, bsend_sem, brecv_sem,
):
    me = lax.axis_index("ctx")
    my_head = lax.axis_index("head")
    nxt = lax.rem(me + 1, owners)
    prv = lax.rem(me + owners - 1, owners)
    pairs = heads // 2
    each = CLUSTERS // owners
    slot_rows = owners * SLOTS * 2 * each
    pair_rows = 2 * rows

    barrier = pltpu.get_barrier_semaphore()

    def greet(i, c):
        pl.semaphore_signal(barrier, inc=1, device_id={"ctx": lax.rem(me + i, owners)}, device_id_type=MESH)
        return c

    lax.fori_loop(1, owners, greet, 0)
    for i in range(1, peers):
        pl.semaphore_signal(barrier, inc=1, device_id={"head": lax.rem(my_head + i, peers)}, device_id_type=MESH)
    pl.semaphore_wait(barrier, owners - 1 + peers - 1)

    id_copies = []
    for i in range(1, peers):
        peer = lax.rem(my_head + i, peers)
        copy = pltpu.make_async_remote_copy(
            src_ref=ids_ref.at[peer], dst_ref=idr.at[i - 1],
            send_sem=id_sem.at[0, i - 1], recv_sem=id_sem.at[1, i - 1],
            device_id={"head": peer}, device_id_type=MESH,
        )
        copy.start()
        id_copies.append(copy)
    halo_copies = []
    for i, ref in enumerate((k_ref, v_ref)):
        copy = pltpu.make_async_remote_copy(
            src_ref=ref, dst_ref=halo.at[i], send_sem=halo_sem.at[0, i], recv_sem=halo_sem.at[1, i],
            device_id={"ctx": nxt}, device_id_type=MESH,
        )
        copy.start()
        halo_copies.append(copy)
    for copy in id_copies:
        copy.wait()
    ids = ids_ref[my_head]
    for i in range(1, peers):
        ids = ids + idr[i - 1]
    head_row = lax.broadcasted_iota(jnp.int32, (heads, rows), 0)
    spot = (ids * (1 + 36 * head_row)) & (CLUSTERS - 1)
    eye = (
        lax.broadcasted_iota(jnp.int32, (rows, rows), 0) == lax.broadcasted_iota(jnp.int32, (rows, rows), 1)
    ).astype(BF16)
    spot_t = nt(eye, spot.astype(F32).astype(BF16)).astype(jnp.int32)
    for h in range(heads):
        crow[h] = spot[h : h + 1, :]
        ccol[h] = spot_t[:, h : h + 1]

    sub_tok = lax.broadcasted_iota(jnp.int32, (rows, rows), 0)
    lane_tok = lax.broadcasted_iota(jnp.int32, (rows, rows), 1)

    def place(spots, rank, hh):
        return (spots // each) * (SLOTS * 2 * each) + rank * (2 * each) + hh * each + spots % each

    def columns(h):
        return pl.ds(pl.multiple_of(h * HEAD_DIM, HEAD_DIM), HEAD_DIM)

    def build(p, c):
        lanes, tokens = [], []
        for hh in range(2):
            h = 2 * p + hh
            row, col = crow[h], ccol[h]
            same = col == row
            rank_row = jnp.sum(jnp.where(same & (sub_tok < lane_tok), 1.0, 0.0), axis=0, keepdims=True)
            rank_col = jnp.sum(jnp.where(same & (lane_tok < sub_tok), 1.0, 0.0), axis=1, keepdims=True)
            lanes.append(place(row, rank_row.astype(jnp.int32), hh))
            tcol[h] = place(col, rank_col.astype(jnp.int32), hh)
            tokens.append(jnp.concatenate([r[:, columns(h)] for r in (q_ref, k_ref, v_ref, g_ref)], axis=1))
        lane = jnp.concatenate(lanes, axis=1)
        token = jnp.concatenate(tokens, axis=0)
        hit = lax.broadcasted_iota(jnp.int32, (slot_rows, pair_rows), 0) == lane
        one_hot = jnp.where(hit, 1.0, 0.0)
        empty = jnp.where(jnp.sum(one_hot, axis=1, keepdims=True) > 0.5, 0.0, EMPTY_KEY)
        filled = nn(one_hot.astype(BF16), token)
        key_lane = lax.broadcasted_iota(jnp.int32, (1, 4 * HEAD_DIM), 1)
        mark = jnp.where((key_lane >= HEAD_DIM) & (key_lane < 2 * HEAD_DIM), 1.0, 0.0)
        filled = filled + empty * mark
        sbuf[p] = filled.astype(BF16).reshape(owners, SLOTS, 2 * each, 4 * HEAD_DIM)

        def send(i, c):
            dst = lax.rem(me + i, owners)
            pltpu.make_async_remote_copy(
                src_ref=sbuf.at[p, dst], dst_ref=rbuf.at[p, me], send_sem=send_sem.at[p], recv_sem=recv_sem.at[p],
                device_id={"ctx": dst}, device_id_type=MESH,
            ).start()
            return c

        lax.fori_loop(1, owners, send, 0)
        pltpu.make_async_copy(sbuf.at[p, me], rbuf.at[p, me], recv_sem.at[p]).start()
        return c

    lax.fori_loop(0, pairs, build, 0)

    for copy in halo_copies:
        copy.wait()
    q_pos = lax.broadcasted_iota(jnp.int32, (rows, WINDOW + rows), 0)
    k_pos = lax.broadcasted_iota(jnp.int32, (rows, WINDOW + rows), 1) - WINDOW
    in_window = (k_pos <= q_pos) & (k_pos > q_pos - WINDOW) & (k_pos + me * rows >= 0)

    def window(h, c):
        cols = columns(h)
        key_all = jnp.concatenate([halo[0, :, cols], k_ref[:, cols]], axis=0)
        value_all = jnp.concatenate([halo[1, :, cols], v_ref[:, cols]], axis=0)
        att, gq, gk, gv = attend(q_ref[:, cols], key_all, value_all, g_ref[:, cols], in_window)
        win[0, :, cols] = att
        win[1, :, cols] = gq
        win[2, :, cols] = gk[WINDOW:]
        win[3, :, cols] = gv[WINDOW:]
        hsend[0, :, cols] = gk[:WINDOW].astype(BF16)
        hsend[1, :, cols] = gv[:WINDOW].astype(BF16)
        return c

    lax.fori_loop(0, heads, window, 0)
    back_copies = []
    for i in range(2):
        copy = pltpu.make_async_remote_copy(
            src_ref=hsend.at[i], dst_ref=hrecv.at[i], send_sem=hback_sem.at[0, i], recv_sem=hback_sem.at[1, i],
            device_id={"ctx": prv}, device_id_type=MESH,
        )
        copy.start()
        back_copies.append(copy)

    groups = 2 * each
    part = owners * groups
    p_row = lax.broadcasted_iota(jnp.int32, (part, part), 0)
    p_col = lax.broadcasted_iota(jnp.int32, (part, part), 1)
    to_group = jnp.where(p_col == (p_row % owners) * groups + p_row // owners, 1.0, 0.0).astype(BF16)
    from_group = jnp.where(p_col == (p_row % groups) * owners + p_row // groups, 1.0, 0.0).astype(BF16)
    capacity = owners * SLOTS
    a_pos = lax.broadcasted_iota(jnp.int32, (capacity, capacity), 0)
    b_pos = lax.broadcasted_iota(jnp.int32, (capacity, capacity), 1)
    causal = (b_pos % owners) * SLOTS + b_pos // owners <= (a_pos % owners) * SLOTS + a_pos // owners
    first = jnp.where(lax.broadcasted_iota(jnp.int32, (8, HEAD_DIM), 1) == 0, 1.0, 0.0).astype(BF16)

    def cluster(p, c):
        pltpu.make_async_copy(rbuf.at[p], rbuf.at[p], recv_sem.at[p]).wait()
        slots = [
            nn(to_group, rbuf[p, :, r].reshape(part, 4 * HEAD_DIM)).astype(BF16) for r in range(SLOTS)
        ]
        results = [[], []]
        for g in range(groups):
            packed = jnp.concatenate([s[g * owners : (g + 1) * owners] for s in slots], axis=0)
            query, key, value, grad = (packed[:, i * HEAD_DIM : (i + 1) * HEAD_DIM] for i in range(4))
            valid = nt(first, key)[0:1, :] < EMPTY_KEY / 2
            done = attend(query, key, value, grad, causal & valid)
            done = jnp.concatenate([d.astype(BF16) for d in done], axis=1)
            for r in range(SLOTS):
                results[r].append(done[r * owners : (r + 1) * owners])
        for r in range(SLOTS):
            back = nn(from_group, jnp.concatenate(results[r], axis=0)).astype(BF16)
            bsend[p, :, r] = back.reshape(owners, groups, 4 * HEAD_DIM)

        def send(i, c):
            dst = lax.rem(me + i, owners)
            pltpu.make_async_remote_copy(
                src_ref=bsend.at[p, dst], dst_ref=brecv.at[p, me], send_sem=bsend_sem.at[p],
                recv_sem=brecv_sem.at[p], device_id={"ctx": dst}, device_id_type=MESH,
            ).start()
            return c

        lax.fori_loop(1, owners, send, 0)
        pltpu.make_async_copy(bsend.at[p, me], brecv.at[p, me], brecv_sem.at[p]).start()
        return c

    lax.fori_loop(0, pairs, cluster, 0)

    for copy in back_copies:
        copy.wait()

    def finish(p, c):
        pltpu.make_async_copy(brecv.at[p], brecv.at[p], brecv_sem.at[p]).wait()
        target = jnp.concatenate([tcol[2 * p], tcol[2 * p + 1]], axis=0)
        hit = lax.broadcasted_iota(jnp.int32, (pair_rows, slot_rows), 1) == target
        mine = nn(jnp.where(hit, 1.0, 0.0).astype(BF16), brecv[p].reshape(slot_rows, 4 * HEAD_DIM))
        for hh in range(2):
            cols = columns(2 * p + hh)
            part_of = [mine[hh * rows : (hh + 1) * rows, i * HEAD_DIM : (i + 1) * HEAD_DIM] for i in range(4)]
            out_o[:, cols] = (win[0, :, cols] + part_of[0]).astype(BF16)
            out_q[:, cols] = (win[1, :, cols] + part_of[1]).astype(BF16)
            out_k[:, cols] = (win[2, :, cols] + hrecv[0, :, cols].astype(F32) + part_of[2]).astype(BF16)
            out_v[:, cols] = (win[3, :, cols] + hrecv[1, :, cols].astype(F32) + part_of[3]).astype(BF16)
        return c

    lax.fori_loop(0, pairs, finish, 0)

    def drain(p, c):
        pltpu.make_async_copy(sbuf.at[p, pl.ds(0, owners - 1)], sbuf.at[p, pl.ds(0, owners - 1)], send_sem.at[p]).wait()
        pltpu.make_async_copy(bsend.at[p, pl.ds(0, owners - 1)], bsend.at[p, pl.ds(0, owners - 1)], bsend_sem.at[p]).wait()
        return c

    lax.fori_loop(0, pairs, drain, 0)


TABLE = (1, 37, 91, 151, 203, 117, 173, 55)
LINE = 8
FIRST_CAP = 40
NEXT_CAP = 80
META = 128


def kernel(
    owners, peers, heads, rows,
    q_hbm, k_hbm, v_hbm, g_hbm, ids_ref,
    out_o, out_q, out_k, out_v, out_flag,
    q_ref, k_ref, v_ref, g_ref, win, r4, ecol,
    sbuf, rbuf, bsend, brecv, halo, stat, stat_send, stat_recv, idr, crow, ccol, trow, tcol, erow,
    acc, e1, r1, e2, r2, back_acc, e3, r3, e4, relay_row, expand_row, flag_out, flag_y, flag_in,
    id_sem, halo_sem, stat_sem, send_sem, recv_sem, bsend_sem, brecv_sem, e_send, e_recv, fy_sem, f_send, f_recv, in_sem,
):
    me = lax.axis_index("ctx")
    my_head = lax.axis_index("head")
    nxt = lax.rem(me + 1, owners)
    prv = lax.rem(me + owners - 1, owners)
    my_x, my_z, my_c = me // 16, (me // 2) % LINE, me % 2
    my_w = my_x * 2 + my_c
    pairs = heads // 2
    each = CLUSTERS // owners
    groups = 2 * each
    part = owners * groups
    pair_rows = 2 * rows
    wide = 4 * HEAD_DIM
    first_rows, next_rows = LINE * FIRST_CAP, LINE * NEXT_CAP

    loads = [
        pltpu.make_async_copy(src, dst, in_sem.at[i])
        for i, (src, dst) in enumerate(((k_hbm, k_ref), (v_hbm, v_ref), (q_hbm, q_ref), (g_hbm, g_ref)))
    ]
    for load in loads:
        load.start()
    barrier = pltpu.get_barrier_semaphore()

    def greet(i, c):
        far = lax.rem(i + owners // 2 + 7, owners - 1) + 1
        pl.semaphore_signal(barrier, inc=1, device_id={"ctx": lax.rem(me + far, owners)}, device_id_type=MESH)
        return c

    lax.fori_loop(0, owners - 1, greet, 0)
    for i in range(1, peers):
        pl.semaphore_signal(barrier, inc=1, device_id={"head": lax.rem(my_head + i, peers)}, device_id_type=MESH)
    pl.semaphore_wait(barrier, owners - 1 + peers - 1)

    id_copies = []
    for i in range(1, peers):
        peer = lax.rem(my_head + i, peers)
        copy = pltpu.make_async_remote_copy(
            src_ref=ids_ref.at[peer], dst_ref=idr.at[i - 1],
            send_sem=id_sem.at[0, i - 1], recv_sem=id_sem.at[1, i - 1],
            device_id={"head": peer}, device_id_type=MESH,
        )
        copy.start()
        id_copies.append(copy)
    for load in loads:
        load.wait()
    halo_copies = []
    for i, ref in enumerate((k_ref, v_ref, q_ref, g_ref)):
        copy = pltpu.make_async_remote_copy(
            src_ref=ref, dst_ref=halo.at[i], send_sem=halo_sem.at[0, i], recv_sem=halo_sem.at[1, i],
            device_id={"ctx": nxt if i < 2 else prv}, device_id_type=MESH,
        )
        copy.start()
        halo_copies.append(copy)
    sub_tok = lax.broadcasted_iota(jnp.int32, (rows, rows), 0)
    lane_tok = lax.broadcasted_iota(jnp.int32, (rows, rows), 1)
    eye = jnp.where(sub_tok == lane_tok, 1.0, 0.0).astype(BF16)
    before = jnp.where(sub_tok < lane_tok, 1.0, 0.0).astype(BF16)
    head_row = lax.broadcasted_iota(jnp.int32, (heads, rows), 0)
    factor = jnp.zeros((heads, rows), jnp.int32)
    for h in range(heads):
        factor = jnp.where(head_row == h, TABLE[h % 8], factor)
    for copy in id_copies:
        copy.wait()
    ids = ids_ref[my_head]
    for i in range(1, peers):
        ids = ids + idr[i - 1]
    spot = (ids * factor + 29 * head_row) & (CLUSTERS - 1)
    spot_t = nt(eye, spot.astype(F32).astype(BF16)).astype(jnp.int32)
    for h in range(heads):
        crow[h] = spot[h : h + 1, :]
        ccol[h] = spot_t[:, h : h + 1]

    def columns(h):
        return pl.ds(pl.multiple_of(h * HEAD_DIM, HEAD_DIM), HEAD_DIM)

    def tokens_of(h):
        return jnp.concatenate([r[:, columns(h)] for r in (q_ref, k_ref, v_ref, g_ref)], axis=1)

    def line_of(spots):
        return (spots // each // 2) % LINE

    line_row = lax.broadcasted_iota(jnp.int32, (LINE, rows), 0)

    def rank(h, used):
        row, col = crow[h], ccol[h]
        same = col == row
        rank_row = jnp.sum(jnp.where(same & (sub_tok < lane_tok), 1.0, 0.0), axis=0, keepdims=True)
        rank_col = jnp.sum(jnp.where(same & (lane_tok < sub_tok), 1.0, 0.0), axis=1, keepdims=True)
        base = (h % 2) * each
        trow[h] = jnp.where(rank_row < 0.5, row // each * groups + base + row % each, -1)
        tcol[h] = jnp.where(rank_col < 0.5, col // each * groups + base + col % each, -1)
        chosen = jnp.where((line_row == line_of(row)) & (rank_row > 0.5), 1.0, 0.0)
        ahead = nn(chosen.astype(BF16), before) + used
        spot_in = jnp.sum(chosen * ahead, axis=0, keepdims=True)
        spot_in = jnp.where(rank_row > 0.5, jnp.minimum(spot_in, 250.0), 250.0)
        erow[h] = spot_in.astype(jnp.int32)
        spot_col = nt(eye, jnp.broadcast_to(spot_in, (8, rows)).astype(BF16))[:, 0:1].astype(jnp.int32)
        ecol[h] = jnp.where(spot_col < FIRST_CAP, line_of(col) * FIRST_CAP + spot_col, -1)
        return used + jnp.sum(chosen, axis=1, keepdims=True)

    used = lax.fori_loop(0, 2, rank, jnp.zeros((LINE, 1), F32))

    lane_wide = lax.broadcasted_iota(jnp.int32, (1, wide), 1)
    key_mark = jnp.where((lane_wide >= HEAD_DIM) & (lane_wide < 2 * HEAD_DIM), 1.0, 0.0)

    def build(p, c):
        lane = jnp.concatenate([trow[2 * p], trow[2 * p + 1]], axis=1)
        token = jnp.concatenate([tokens_of(2 * p), tokens_of(2 * p + 1)], axis=0)
        one_hot = jnp.where(lax.broadcasted_iota(jnp.int32, (part, pair_rows), 0) == lane, 1.0, 0.0)
        empty = jnp.where(jnp.sum(one_hot, axis=1, keepdims=True) > 0.5, 0.0, EMPTY_KEY)
        filled = nn(one_hot.astype(BF16), token) + empty * key_mark
        sbuf[p] = filled.astype(BF16).reshape(owners, groups, wide)

        def send(i, c):
            dst = lax.rem(me + i, owners)
            pltpu.make_async_remote_copy(
                src_ref=sbuf.at[p, dst], dst_ref=rbuf.at[p, me], send_sem=send_sem.at[p], recv_sem=recv_sem.at[p],
                device_id={"ctx": dst}, device_id_type=MESH,
            ).start()
            return c

        lax.fori_loop(1, owners, send, 0)
        pltpu.make_async_copy(sbuf.at[p, me], rbuf.at[p, me], recv_sem.at[p]).start()
        return c

    def along_z(stage, src, dst):
        def send(i, c):
            z = lax.rem(my_z + i, LINE)
            pltpu.make_async_remote_copy(
                src_ref=src.at[z], dst_ref=dst.at[my_z], send_sem=e_send.at[stage], recv_sem=e_recv.at[stage],
                device_id={"ctx": my_x * 16 + z * 2 + my_c}, device_id_type=MESH,
            ).start()
            return c

        lax.fori_loop(1, LINE, send, 0)
        pltpu.make_async_copy(src.at[my_z], dst.at[my_z], e_recv.at[stage]).start()

    def across(stage, src, dst):
        def send(i, c):
            w = lax.rem(my_w + i, LINE)
            pltpu.make_async_remote_copy(
                src_ref=src.at[w], dst_ref=dst.at[my_w], send_sem=e_send.at[stage], recv_sem=e_recv.at[stage],
                device_id={"ctx": w // 2 * 16 + my_z * 2 + w % 2}, device_id_type=MESH,
            ).start()
            return c

        lax.fori_loop(1, LINE, send, 0)
        pltpu.make_async_copy(src.at[my_w], dst.at[my_w], e_recv.at[stage]).start()

    def arrived(stage, dst):
        pltpu.make_async_copy(dst, dst, e_recv.at[stage]).wait()

    build(0, 0)
    used = lax.fori_loop(2, heads, rank, used)
    spill = jnp.max(used, axis=0, keepdims=True) - FIRST_CAP

    lane_meta = lax.broadcasted_iota(jnp.int32, (rows, META), 1)
    acc[...] = jnp.zeros_like(acc)

    def second(h, c):
        place = erow[h]
        target = jnp.where(place < FIRST_CAP, line_of(crow[h]) * FIRST_CAP + place, -1)
        one_hot = jnp.where(lax.broadcasted_iota(jnp.int32, (first_rows, rows), 0) == target, 1.0, 0.0).astype(BF16)
        meta = jnp.where(lane_meta == 0, ccol[h], jnp.where(lane_meta == 1, h, jnp.where(lane_meta == 2, me, 1)))
        meta = jnp.where(lane_meta < 4, meta, 0).astype(F32).astype(BF16)
        acc[...] += nn(one_hot, jnp.concatenate([tokens_of(h), meta], axis=1))
        return c

    lax.fori_loop(0, heads, second, 0)
    e1[...] = acc[...].astype(BF16).reshape(LINE, FIRST_CAP, wide + META)
    along_z(0, e1, r1)

    build(1, 0)

    for copy in halo_copies[:2]:
        copy.wait()
    q_pos = lax.broadcasted_iota(jnp.int32, (rows, WINDOW + rows), 0)
    k_pos = lax.broadcasted_iota(jnp.int32, (rows, WINDOW + rows), 1) - WINDOW
    in_window = (k_pos <= q_pos) & (k_pos > q_pos - WINDOW) & (k_pos + me * rows >= 0)
    lane_stat = lax.broadcasted_iota(jnp.int32, (rows, META), 1)

    def window(h, c):
        cols = columns(h)
        query, grad = q_ref[:, cols], g_ref[:, cols]
        key_all = jnp.concatenate([halo[0, :, cols], k_ref[:, cols]], axis=0)
        value_all = jnp.concatenate([halo[1, :, cols], v_ref[:, cols]], axis=0)
        scores = jnp.where(in_window, nt(query, key_all) * SCALE, NEG_LARGE)
        top = jnp.max(scores, axis=-1, keepdims=True)
        exps = jnp.where(in_window, jnp.exp(scores - top), 0.0)
        inverse = 1.0 / jnp.sum(exps, axis=-1, keepdims=True)
        weights16 = (exps * inverse).astype(BF16)
        attended = nn(weights16, value_all)
        row_dot = jnp.sum(grad.astype(F32) * attended, axis=-1, keepdims=True)
        grad_scores = (weights16.astype(F32) * (nt(grad, value_all) - row_dot)).astype(BF16)
        win[0, :, cols] = attended
        win[1, :, cols] = nn(grad_scores, key_all) * SCALE
        win[2, :, cols] = tn(grad_scores[:, WINDOW:], query) * SCALE
        win[3, :, cols] = tn(weights16[:, WINDOW:], grad)
        old = jnp.where(lane_stat == h, top, stat[...])
        stat[...] = jnp.where(lane_stat == heads + h, inverse, jnp.where(lane_stat == 2 * heads + h, row_dot, old))
        return c

    stat[...] = jnp.zeros_like(stat)
    lax.fori_loop(0, heads, window, 0)
    stat_send[...] = stat[...].T[: 4 * heads].reshape(4 * heads, 1, rows)
    stat_copy = pltpu.make_async_remote_copy(
        src_ref=stat_send, dst_ref=stat_recv, send_sem=stat_sem.at[0], recv_sem=stat_sem.at[1],
        device_id={"ctx": prv}, device_id_type=MESH,
    )
    stat_copy.start()

    lax.fori_loop(2, pairs - 1, build, 0)

    arrived(0, r1)
    pick = jnp.where(
        lax.broadcasted_iota(jnp.int32, (8, META), 0) == lax.broadcasted_iota(jnp.int32, (8, META), 1), 1.0, 0.0
    ).astype(BF16)
    came = r1[...].reshape(first_rows, wide + META)
    labels = nt(pick, came[:, wide:])
    owner = labels[0:1].astype(jnp.int32) // each
    live = labels[3:4] > 0.5
    across_row = lax.broadcasted_iota(jnp.int32, (LINE, first_rows), 0)
    chosen = jnp.where((across_row == owner // 16 * 2 + owner % 2) & live, 1.0, 0.0)
    earlier = jnp.where(
        lax.broadcasted_iota(jnp.int32, (first_rows, first_rows), 0)
        < lax.broadcasted_iota(jnp.int32, (first_rows, first_rows), 1), 1.0, 0.0,
    ).astype(BF16)
    place = jnp.sum(chosen * nn(chosen.astype(BF16), earlier), axis=0, keepdims=True).astype(jnp.int32)
    target = jnp.where(live & (place < NEXT_CAP), (owner // 16 * 2 + owner % 2) * NEXT_CAP + place, -1)
    relay_row[...] = target
    count = jnp.max(jnp.sum(chosen, axis=1, keepdims=True), axis=0, keepdims=True)
    spill = jnp.maximum(spill, count - NEXT_CAP)
    flag_out[0] = jnp.broadcast_to(jnp.where(spill > 0.5, 1.0, 0.0), (1, META))

    def relay_hot():
        hit = lax.broadcasted_iota(jnp.int32, (next_rows, first_rows), 0) == relay_row[...]
        return jnp.where(hit, 1.0, 0.0).astype(BF16)

    e2[...] = nn(relay_hot(), came).astype(BF16).reshape(LINE, NEXT_CAP, wide + META)
    across(1, e2, r2)

    flag_copies = []
    for i in range(1, peers):
        copy = pltpu.make_async_remote_copy(
            src_ref=flag_out.at[0], dst_ref=flag_y.at[i - 1], send_sem=fy_sem.at[0, i - 1],
            recv_sem=fy_sem.at[1, i - 1], device_id={"head": lax.rem(my_head + i, peers)}, device_id_type=MESH,
        )
        copy.start()
        flag_copies.append(copy)
    build(pairs - 1, 0)

    arrived(1, r2)
    guests = r2[...].reshape(next_rows, wide + META)
    labels = nt(pick, guests[:, wide:]).astype(jnp.int32)
    spots, whose, block, live = labels[0:1], labels[1:2], labels[2:3], labels[3:4]
    for p in range(pairs):
        seat = ((whose % 2) * each + spots % each) * owners + block
        expand_row[p] = jnp.where((live > 0) & (whose // 2 == p), seat, -1)
    p_row = lax.broadcasted_iota(jnp.int32, (part, part), 0)
    p_col = lax.broadcasted_iota(jnp.int32, (part, part), 1)
    to_group = jnp.where(p_col == (p_row % owners) * groups + p_row // owners, 1.0, 0.0).astype(BF16)
    from_group = jnp.where(p_col == (p_row % groups) * owners + p_row // groups, 1.0, 0.0).astype(BF16)
    capacity = owners * SLOTS
    a_pos = lax.broadcasted_iota(jnp.int32, (capacity, capacity), 0)
    b_pos = lax.broadcasted_iota(jnp.int32, (capacity, capacity), 1)
    causal = (b_pos % owners) * SLOTS + b_pos // owners <= (a_pos % owners) * SLOTS + a_pos // owners
    first = jnp.where(lax.broadcasted_iota(jnp.int32, (8, HEAD_DIM), 1) == 0, 1.0, 0.0).astype(BF16)
    back_acc[...] = jnp.zeros_like(back_acc)

    def give(p):
        def send(i, c):
            dst = lax.rem(me + i, owners)
            pltpu.make_async_remote_copy(
                src_ref=bsend.at[p, dst], dst_ref=brecv.at[p, me], send_sem=bsend_sem.at[p],
                recv_sem=brecv_sem.at[p], device_id={"ctx": dst}, device_id_type=MESH,
            ).start()
            return c

        lax.fori_loop(1, owners, send, 0)
        pltpu.make_async_copy(bsend.at[p, me], brecv.at[p, me], brecv_sem.at[p]).start()

    def cluster(p, c):
        pltpu.make_async_copy(rbuf.at[p], rbuf.at[p], recv_sem.at[p]).wait()
        hit = lax.broadcasted_iota(jnp.int32, (part, next_rows), 0) == expand_row[p]
        seats = jnp.where(hit, 1.0, 0.0)
        empty = jnp.where(jnp.sum(seats, axis=1, keepdims=True) > 0.5, 0.0, EMPTY_KEY)
        seats = seats.astype(BF16)
        guest = r2[...].reshape(next_rows, wide + META)[:, :wide]
        slots = [
            nn(to_group, rbuf[p].reshape(part, wide)).astype(BF16),
            (nn(seats, guest) + empty * key_mark).astype(BF16),
        ]
        packed = [
            jnp.concatenate([one[g * owners : (g + 1) * owners] for one in slots], axis=0) for g in range(groups)
        ]
        allowed = jnp.concatenate(
            [causal & (nt(first, one[:, HEAD_DIM : 2 * HEAD_DIM])[0:1, :] < EMPTY_KEY / 2) for one in packed], axis=0
        )
        done = attend_groups(packed, allowed)
        results = [[one[r * owners : (r + 1) * owners] for one in done] for r in range(SLOTS)]
        back = nn(from_group, jnp.concatenate(results[0], axis=0)).astype(BF16)
        bsend[p] = back.reshape(owners, groups, wide)
        pl.when(p < pairs - 1)(lambda: give(p))

        back_acc[...] += tn(seats, jnp.concatenate(results[1], axis=0))
        return c

    lax.fori_loop(0, pairs, cluster, 0)
    e3[...] = back_acc[...].astype(BF16).reshape(LINE, NEXT_CAP, wide)
    across(2, e3, r3)
    for copy in flag_copies:
        copy.wait()
    raised = flag_out[0]
    for i in range(1, peers):
        raised = jnp.maximum(raised, flag_y[i - 1])
    flag_out[1] = raised

    def tell(i, c):
        dst = lax.rem(me + i, owners)
        pltpu.make_async_remote_copy(
            src_ref=flag_out.at[1], dst_ref=flag_in.at[me], send_sem=f_send, recv_sem=f_recv,
            device_id={"ctx": dst}, device_id_type=MESH,
        ).start()
        return c

    lax.fori_loop(1, owners, tell, 0)
    pltpu.make_async_copy(flag_out.at[1], flag_in.at[me], f_recv).start()

    for copy in halo_copies[2:]:
        copy.wait()
    stat_copy.wait()
    seen = (sub_tok > lane_tok) & (me < owners - 1)

    def ahead(h, c):
        cols = columns(h)
        query, grad = halo[2, :, cols], halo[3, :, cols]
        scores = nt(k_ref[:, cols], query) * SCALE
        exps = jnp.exp(jnp.where(seen, scores - stat_recv[h], NEG_LARGE))
        weights16 = (exps * stat_recv[heads + h]).astype(BF16)
        change = nt(v_ref[:, cols], grad) - stat_recv[2 * heads + h]
        grad_scores = (weights16.astype(F32) * change).astype(BF16)
        win[2, :, cols] += nn(grad_scores, query) * SCALE
        win[3, :, cols] += nn(weights16, grad)
        return c

    lax.fori_loop(0, heads, ahead, 0)
    arrived(2, r3)
    e4[...] = tn(relay_hot(), r3[...].reshape(next_rows, wide)).astype(BF16).reshape(LINE, FIRST_CAP, wide)
    along_z(3, e4, r4)
    give(pairs - 1)


    outs = (out_o, out_q, out_k, out_v)

    def settle(p):
        pltpu.make_async_copy(brecv.at[p], brecv.at[p], brecv_sem.at[p]).wait()
        target = jnp.concatenate([tcol[2 * p], tcol[2 * p + 1]], axis=0)
        hit = lax.broadcasted_iota(jnp.int32, (pair_rows, part), 1) == target
        mine = nn(jnp.where(hit, 1.0, 0.0).astype(BF16), brecv[p].reshape(part, wide))
        for hh in range(2):
            cols = columns(2 * p + hh)
            for i in range(4):
                both = win[i, :, cols] + mine[hh * rows : (hh + 1) * rows, i * HEAD_DIM : (i + 1) * HEAD_DIM]
                yield i, cols, both

    def settle_in(p, c):
        for i, cols, both in settle(p):
            win[i, :, cols] = both
        return c

    lax.fori_loop(0, pairs - 1, settle_in, 0)
    arrived(3, r4)

    def late(h):
        hit = lax.broadcasted_iota(jnp.int32, (rows, first_rows), 1) == ecol[h]
        mine = nn(jnp.where(hit, 1.0, 0.0).astype(BF16), r4[...].reshape(first_rows, wide))
        return [win[i, :, columns(h)] + mine[:, i * HEAD_DIM : (i + 1) * HEAD_DIM] for i in range(4)]

    def late_in(h, c):
        for i, both in enumerate(late(h)):
            win[i, :, columns(h)] = both
        return c

    def late_out(h, c):
        for i, both in enumerate(late(h)):
            outs[i][:, columns(h)] = both.astype(BF16)
        return c

    lax.fori_loop(heads - 2, heads, late_in, 0)
    lax.fori_loop(0, heads - 2, late_out, 0)
    for i, cols, both in settle(pairs - 1):
        outs[i][:, cols] = both.astype(BF16)
    pltpu.make_async_copy(flag_in, flag_in, f_recv).wait()
    out_flag[...] = jnp.max(flag_in[...], axis=0)

    def drain(p, c):
        some = pl.ds(0, owners - 1)
        pltpu.make_async_copy(sbuf.at[p, some], sbuf.at[p, some], send_sem.at[p]).wait()
        pltpu.make_async_copy(bsend.at[p, some], bsend.at[p, some], bsend_sem.at[p]).wait()
        return c

    lax.fori_loop(0, pairs, drain, 0)
    some = pl.ds(0, LINE - 1)
    for stage, ref in enumerate((e1, e2, e3, e4)):
        pltpu.make_async_copy(ref.at[some], ref.at[some], e_send.at[stage]).wait()
    some = pl.ds(0, owners - 1)
    pltpu.make_async_copy(flag_in.at[some], flag_in.at[some], f_send).wait()


def finish_kernel(*refs):
    p = pl.program_id(0)
    for src, out in zip(refs[:4], refs[4:]):
        size = out.shape[0]
        out[...] = src[pl.ds(pl.multiple_of(p * size, size), size), :]


def on_device(queries, keys, values, grad_out, cluster_ids):
    rows, width = queries.shape
    heads = width // HEAD_DIM
    owners = lax.axis_size("ctx")
    peers = lax.axis_size("head")
    each = CLUSTERS // owners
    share = rows // peers
    ids = cluster_ids[:, :, 0].reshape(peers, heads, share)
    spread = jnp.zeros((peers, heads, rows), jnp.int32)
    spread = lax.dynamic_update_slice_in_dim(spread, ids, lax.axis_index("head") * share, axis=2)
    pairs = heads // 2
    vmem = pl.BlockSpec(memory_space=pltpu.VMEM)
    dma = pltpu.SemaphoreType.DMA
    args = (queries, keys, values, grad_out, spread)
    result = jax.ShapeDtypeStruct((rows, width), BF16)
    wide = 4 * HEAD_DIM

    anywhere = pl.BlockSpec(memory_space=pl.ANY)

    def call(body, outs, scratch, number, ins=None, places=None):
        return pl.pallas_call(
            functools.partial(body, owners, peers, heads, rows),
            out_shape=outs,
            in_specs=ins or [vmem] * 5,
            out_specs=places or [vmem] * len(outs),
            scratch_shapes=scratch,
            compiler_params=pltpu.CompilerParams(
                collective_id=number, has_side_effects=True, vmem_limit_bytes=36 * 1024 * 1024
            ),
        )(*args)

    buffer = pltpu.VMEM((pairs, owners, SLOTS, 2 * each, wide), BF16)
    narrow = pltpu.VMEM((pairs, owners, 2 * each, wide), BF16)
    window = [pltpu.VMEM((2, WINDOW, width), BF16)] * 3
    total = pltpu.VMEM((4, rows, width), F32)
    row_list = pltpu.VMEM((heads, 1, rows), jnp.int32)
    col_list = pltpu.VMEM((heads, rows, 1), jnp.int32)
    ids_in = pltpu.VMEM((peers - 1, heads, rows), jnp.int32)
    sems = [dma((2, peers - 1)), dma((2, 2)), dma((2, 2)), dma((pairs,)), dma((pairs,)), dma((pairs,)), dma((pairs,))]

    def line(cap, size):
        return pltpu.VMEM((LINE, cap, size), BF16)

    *outs, flag = call(
        kernel,
        [result] * 4 + [jax.ShapeDtypeStruct((1, META), F32)],
        [pltpu.VMEM((rows, width), BF16)] * 4 + [total, line(FIRST_CAP, wide), col_list] + [narrow] * 4
        + [pltpu.VMEM((4, WINDOW, width), BF16), pltpu.VMEM((rows, META), F32)]
        + [pltpu.VMEM((4 * heads, 1, rows), F32)] * 2
        + [ids_in, row_list, col_list, row_list, col_list, row_list]
        + [pltpu.VMEM((LINE * FIRST_CAP, wide + META), F32)]
        + [line(FIRST_CAP, wide + META)] * 2 + [line(NEXT_CAP, wide + META)] * 2
        + [pltpu.VMEM((LINE * NEXT_CAP, wide), F32)] + [line(NEXT_CAP, wide)] * 2 + [line(FIRST_CAP, wide)]
        + [pltpu.VMEM((1, LINE * FIRST_CAP), jnp.int32), pltpu.VMEM((pairs, 1, LINE * NEXT_CAP), jnp.int32)]
        + [pltpu.VMEM((2, 1, META), F32), pltpu.VMEM((peers - 1, 1, META), F32), pltpu.VMEM((owners, 1, META), F32)]
        + [dma((2, peers - 1)), dma((2, 4)), dma((2,))] + sems[3:] + [dma((4,)), dma((4,)), dma((2, peers - 1)), dma, dma, dma((4,))],
        0,
        [anywhere] * 4 + [vmem],
        [vmem] * 5,
    )

    def again():
        return tuple(
            call(wide_kernel, [result] * 4, [buffer] * 4 + window + [total, ids_in, row_list, col_list, col_list] + sems, 1)
        )

    outs = lax.cond(flag[0, 0] > 0.5, again, lambda: tuple(outs))
    return pl.pallas_call(
        finish_kernel,
        grid=(pairs,),
        out_shape=[result] * 4,
        in_specs=[vmem] * 4,
        out_specs=[pl.BlockSpec((rows // pairs, width), lambda p: (p, 0))] * 4,
        compiler_params=pltpu.CompilerParams(vmem_limit_bytes=24 * 1024 * 1024),
    )(*outs)


def solution(mesh):
    return jax.shard_map(
        on_device,
        mesh=mesh,
        in_specs=(
            P("ctx", "head"), P("ctx", "head"), P("ctx", "head"), P("ctx", "head"),
            P(None, ("ctx", "head"), None),
        ),
        out_specs=(P("ctx", "head"),) * 4,
        check_vma=False,
    )
```
